128 devices in a mesh: rows: 4 (over z), cols: 32 (over x, y, core).
Axes of the slice: x: 4, y: 4, z: 4, core: 2. Of those that a mesh axis runs over, the one named last changes fastest.
Arguments:
- fields: float32 [5, 64, 1024, 512], P(None, None, 'cols', 'rows'), may hold values from -6 to 6
- cotangent: float32 [5, 64, 1024, 512], P(None, None, 'cols', 'rows'), may hold values from -6 to 6
- ocean_mask: int32 [1024, 512], P('cols', 'rows'), may hold values from 0 to 1
- depth_levels: int32 [1024, 512], P('cols', 'rows'), may hold values from 16 to 64
- in_weight: bfloat16 [256, 256], replicated, may hold values from -0.375 to 0.375
- in_bias: float32 [256], replicated, may hold values from -3 to 3
- out_weight: bfloat16 [256, 63], replicated, may hold values from -0.375 to 0.375
Outputs:
- new_fields: float32 [5, 64, 1024, 512], P(None, None, 'cols', 'rows')
- pressure: float32 [64, 1024, 512], P(None, 'cols', 'rows')
- grad_in_weight: float32 [256, 256], replicated
- grad_in_bias: float32 [256], replicated
- grad_out_weight: float32 [256, 63], replicated
The draws below stay inside these ranges and needn't reach their ends.
All inputs are finite; a program needn't handle non-finite values.
Results may differ from the reference program's by a relative error of at most 0.0059.
Values sent between devices are 32-bit elements; how exact they have to be, the bound alone decides.
A program may use at most 192 MiB of HBM per device.

```python
import math
import jax
import jax.numpy as jnp
from jax import lax

NZ = 64
HID = 256
NX = 512
NY = 1024


def draw_ocean_mask(key, part):
    walk_key, island_key = jax.random.split(jax.random.fold_in(key, 11))
    steps_taken = jax.random.randint(walk_key, (NY,), -3, 4)
    coast = jnp.clip(NX // 2 + jnp.cumsum(steps_taken), NX // 8, NX)
    east_ids = jnp.arange(NX)
    shore = east_ids[None, :] < coast[:, None]
    islands = jax.random.randint(island_key, (NY, NX), 0, 8) > 0
    return (shore & islands).astype(jnp.int32)


def draw_cotangent(key, part):
    field_key = jax.random.fold_in(key, 23)
    values = jnp.clip(jax.random.normal(field_key, (5, NZ, NY, NX), jnp.float32), -6.0, 6.0)
    factors = jnp.array([1.0, 1.0, 1.0, 0.01, 0.01], jnp.float32)[:, None, None, None]
    return (values * factors).astype(jnp.float32)


def touch_ends(result, key, least, high):
    place = [jax.random.randint(jax.random.fold_in(key, axis), (), 0, length) for axis, length in enumerate(result.shape)]
    widest = result.shape.index(max(result.shape))
    neighbour = place[:widest] + [(place[widest] + 1) % result.shape[widest]] + place[widest + 1:]
    return result.at[tuple(place)].set(least).at[tuple(neighbour)].set(high)


def level_of(rng, extent, pieces, smallest, top_value):
    def one(axis_at, shards_of):
        heights = jax.random.uniform(jax.random.fold_in(jax.random.fold_in(rng, 6), axis_at), (shards_of,), jnp.float32, smallest / len(pieces), top_value / len(pieces))
        return jnp.repeat(jnp.exp(heights), extent[axis_at] // shards_of).reshape((-1,) + (1,) * (len(extent) - axis_at - 1))

    factor_of = one(*pieces[0])
    for cut in pieces[1:]:
        factor_of = factor_of * one(*cut)
    return factor_of


def centred(own_key, shape, scale, bound, shards=(), kind=jnp.bfloat16):
    factor_of = level_of(own_key, shape, shards, -0.22, 0.18) if shards else 1.0
    values = jax.random.normal(own_key, shape, jnp.float32) * scale * factor_of
    return jnp.minimum(jnp.maximum(values, -bound), bound).astype(kind)


def setup_inputs(seed: int = 0) -> dict:
    key_of = jax.random.split(jax.random.key(seed), 8)
    return {
        "fields": centred(key_of[0], (5, NZ, NY, NX), 1.0, 6.0, ((2, 32), (3, 4)), jnp.float32),
        "cotangent": draw_cotangent(jax.random.fold_in(key_of[7], 71), 0),
        "ocean_mask": draw_ocean_mask(jax.random.fold_in(key_of[7], 71), 0),
        "depth_levels": touch_ends(jax.random.randint(key_of[3], (NY, NX), NZ // 4, NZ + 1), jax.random.fold_in(key_of[3], 1), NZ // 4, NZ).astype(jnp.int32),
        "in_weight": centred(key_of[4], (4 * NZ, HID), (4 * NZ) ** -0.5, 0.375),
        "in_bias": centred(key_of[5], (HID,), 0.5, 3.0, (), jnp.float32),
        "out_weight": centred(key_of[6], (HID, NZ - 1), HID ** -0.5, 0.375),
    }


TIME_STEP = 0.2
RATE_MAX = 2.0
THERMAL = 0.5
HALINE = 0.5
SPECTRAL_SHIFT = 0.001
WENO_EPS = 1e-06

def weno_face(first, second, third, fourth, fifth):
    cand_low = (2.0 * first - 7.0 * second + 11.0 * third) / 6.0
    cand_mid = (-second + 5.0 * third + 2.0 * fourth) / 6.0
    cand_high = (2.0 * third + 5.0 * fourth - fifth) / 6.0
    rough_low = 13.0 / 12.0 * jnp.square(first - 2.0 * second + third) + 0.25 * jnp.square(first - 4.0 * second + 3.0 * third)
    rough_mid = 13.0 / 12.0 * jnp.square(second - 2.0 * third + fourth) + 0.25 * jnp.square(second - fourth)
    rough_high = 13.0 / 12.0 * jnp.square(third - 2.0 * fourth + fifth) + 0.25 * jnp.square(3.0 * third - 4.0 * fourth + fifth)
    weight_low = 0.1 / jnp.square(WENO_EPS + rough_low)
    weight_mid = 0.6 / jnp.square(WENO_EPS + rough_mid)
    weight_high = 0.3 / jnp.square(WENO_EPS + rough_high)
    return (weight_low * cand_low + weight_mid * cand_mid + weight_high * cand_high) / (weight_low + weight_mid + weight_high)

def take_cells(array, start, length, along):
    return lax.slice_in_dim(array, start, start + length, axis=along)

def flux_tendency(tracer, velocity, wet_cells, along, length):
    shifted = [take_cells(tracer, offset, length + 1, along) for offset in range(6)]
    left_value = weno_face(shifted[0], shifted[1], shifted[2], shifted[3], shifted[4])
    right_value = weno_face(shifted[5], shifted[4], shifted[3], shifted[2], shifted[1])
    face_speed = 0.5 * (take_cells(velocity, 2, length + 1, along) + take_cells(velocity, 3, length + 1, along))
    face_speed = face_speed * take_cells(wet_cells, 2, length + 1, along) * take_cells(wet_cells, 3, length + 1, along)
    face_flux = jnp.maximum(face_speed, 0.0) * left_value + jnp.minimum(face_speed, 0.0) * right_value
    return take_cells(face_flux, 0, length, along) - take_cells(face_flux, 1, length, along)

def advect_one(tracer, east_speed, north_speed, wet_cells, north_count, east_count):
    inner_rows = slice(3, 3 + north_count)
    inner_cols = slice(3, 3 + east_count)
    along_east = flux_tendency(tracer[:, inner_rows, :], east_speed[:, inner_rows, :], wet_cells[:, inner_rows, :], 2, east_count)
    along_north = flux_tendency(tracer[:, :, inner_cols], north_speed[:, :, inner_cols], wet_cells[:, :, inner_cols], 1, north_count)
    inner = tracer[:, inner_rows, inner_cols]
    return wet_cells[:, inner_rows, inner_cols] * (inner + TIME_STEP * (along_east + along_north))

def advance(extended, north_count, east_count):
    advected = lax.map(lambda tracer: advect_one(tracer, extended[0], extended[1], extended[5], north_count, east_count), extended[:5])
    east_speed = extended[0]
    north_speed = extended[1]
    east_change = east_speed[:, 3:3 + north_count, 4:4 + east_count] - east_speed[:, 3:3 + north_count, 2:2 + east_count]
    north_change = north_speed[:, 4:4 + north_count, 3:3 + east_count] - north_speed[:, 2:2 + north_count, 3:3 + east_count]
    return (advected, 0.5 * (east_change + north_change))

def wet_mask(ocean_mask, depth_levels):
    level_ids = jnp.arange(NZ, dtype=jnp.int32)[:, None, None]
    wet_cells = (ocean_mask[None] == 1) & (level_ids < depth_levels[None])
    return wet_cells.astype(jnp.float32)

def vertical_diff(array):
    zero_layer = jnp.zeros_like(array[:1])
    upper = jnp.concatenate([array[1:], zero_layer], 0)
    lower = jnp.concatenate([zero_layer, array[:-1]], 0)
    return 0.5 * (upper - lower)

def mix_column(tracer, rates, wet_cells, bond):
    face_flux = rates * bond * (tracer[1:] - tracer[:-1])
    zero_layer = jnp.zeros_like(face_flux[:1])
    padded = jnp.concatenate([zero_layer, face_flux, zero_layer], 0)
    return wet_cells * (tracer + TIME_STEP * (padded[1:] - padded[:-1]))

def rate_gradient(tracer, grad_tracer, wet_cells, bond):
    weighted = wet_cells * grad_tracer
    return TIME_STEP * (weighted[:-1] - weighted[1:]) * bond * (tracer[1:] - tracer[:-1])

def closure_forward(advected, in_weight, in_bias, out_weight):
    levels = advected.shape[1]
    features = jnp.concatenate([advected[0], advected[1], advected[3], advected[4]], 0).reshape(4 * levels, -1).astype(jnp.bfloat16)
    hidden_pre = lax.dot_general(in_weight, features, (((0,), (0,)), ((), ())), preferred_element_type=jnp.float32) + in_bias[:, None]
    activity = jnp.tanh(hidden_pre)
    hidden = activity.astype(jnp.bfloat16)
    output = lax.dot_general(out_weight, hidden, (((0,), (0,)), ((), ())), preferred_element_type=jnp.float32)
    rates = RATE_MAX * jax.nn.sigmoid(output)
    return (features, activity, hidden, rates)

def closure_backward(features, activity, hidden, rates, grad_rates, out_weight):
    grad_output = (grad_rates * rates * (1.0 - rates / RATE_MAX)).astype(jnp.bfloat16)
    grad_w_out = lax.dot_general(hidden, grad_output, (((1,), (1,)), ((), ())), preferred_element_type=jnp.float32)
    grad_pre = jnp.dot(out_weight, grad_output, preferred_element_type=jnp.float32) * (1.0 - activity * activity)
    grad_b_in = lax.optimization_barrier(jnp.sum(grad_pre, axis=1))
    grad_w_in = lax.dot_general(features, grad_pre.astype(jnp.bfloat16), (((1,), (1,)), ((), ())), preferred_element_type=jnp.float32)
    return (grad_w_in, grad_b_in, grad_w_out)

def column_step(advected, masked, wet_cells, spread, cotangent, in_weight, in_bias, out_weight):
    features, activity, hidden, rates_flat = closure_forward(advected, in_weight, in_bias, out_weight)
    rates = rates_flat.reshape(wet_cells.shape[0] - 1, wet_cells.shape[1], wet_cells.shape[2])
    bond = wet_cells[:-1] * wet_cells[1:]
    heat = mix_column(advected[3], rates, wet_cells, bond)
    salt = mix_column(advected[4], rates, wet_cells, bond)
    density = THERMAL * heat - HALINE * salt
    forcing = wet_cells * (vertical_diff(density) - (spread + vertical_diff(masked[2])) / TIME_STEP)
    adjoint_source = TIME_STEP * vertical_diff(wet_cells * cotangent[2])
    saved = (features, activity, hidden, rates_flat, bond, heat, salt)
    return (saved, forcing, adjoint_source)

def finish_step(advected, wet_cells, pressure, back, cotangent, saved, out_weight):
    features, activity, hidden, rates_flat, bond, heat, salt = saved
    new_w = wet_cells * (advected[2] - TIME_STEP * vertical_diff(pressure))
    new_fields = jnp.stack([advected[0], advected[1], new_w, heat, salt])
    grad_density = -vertical_diff(wet_cells * back)
    grad_heat = cotangent[3] + THERMAL * grad_density
    grad_salt = cotangent[4] - HALINE * grad_density
    grad_rates = rate_gradient(advected[3], grad_heat, wet_cells, bond) + rate_gradient(advected[4], grad_salt, wet_cells, bond)
    grads = closure_backward(features, activity, hidden, rates_flat, grad_rates.reshape(rates_flat.shape), out_weight)
    return (new_fields, grads)

def dct_matrix(length):
    freq = jnp.arange(length, dtype=jnp.float32)[:, None]
    cells = jnp.arange(length, dtype=jnp.float32)[None, :]
    scale = jnp.where(freq == 0.0, jnp.sqrt(1.0 / length), jnp.sqrt(2.0 / length))
    return scale * jnp.cos(math.pi * (cells + 0.5) * freq / length)

def eigen_values(freq, length):
    return 2.0 - 2.0 * jnp.cos(math.pi * freq.astype(jnp.float32) / length)

def spectral_solve(source):
    high = lax.Precision.HIGHEST
    level_matrix = dct_matrix(NZ)
    north_matrix = dct_matrix(NY)
    east_matrix = dct_matrix(NX)
    spectrum = jnp.einsum('mz,zyx->myx', level_matrix, source, precision=high)
    spectrum = jnp.einsum('ky,myx->mkx', north_matrix, spectrum, precision=high)
    spectrum = jnp.einsum('myx,kx->myk', spectrum, east_matrix, precision=high)
    denominator = SPECTRAL_SHIFT + eigen_values(jnp.arange(NZ), NZ)[:, None, None] + eigen_values(jnp.arange(NY), NY)[None, :, None] + eigen_values(jnp.arange(NX), NX)[None, None, :]
    spectrum = spectrum / denominator
    spectrum = jnp.einsum('myk,kx->myx', spectrum, east_matrix, precision=high)
    spectrum = jnp.einsum('ky,mkx->myx', north_matrix, spectrum, precision=high)
    return jnp.einsum('mz,myx->zyx', level_matrix, spectrum, precision=high)

def reference(fields, cotangent, ocean_mask, depth_levels, in_weight, in_bias, out_weight):
    wet_cells = wet_mask(ocean_mask, depth_levels)
    masked = fields * wet_cells[None]
    stacked = jnp.concatenate([masked, wet_cells[None]], 0)
    extended = jnp.pad(stacked, ((0, 0), (0, 0), (3, 3), (3, 3)))
    advected, spread = advance(extended, NY, NX)
    saved, forcing, adjoint_source = column_step(advected, masked, wet_cells, spread, cotangent, in_weight, in_bias, out_weight)
    pressure = spectral_solve(forcing)
    back = spectral_solve(adjoint_source)
    new_fields, grads = finish_step(advected, wet_cells, pressure, back, cotangent, saved, out_weight)
    return (new_fields, pressure, grads[0], grads[1], grads[2])
```

```python
import functools
import math

import jax
import jax.numpy as jnp
import numpy as np
from jax import lax
from jax.experimental import pallas as pl
from jax.experimental.pallas import tpu as pltpu
from jax.sharding import PartitionSpec as P

NZ = 64
TIME_STEP = 0.2
SPECTRAL_SHIFT = 0.001
WENO_EPS = 1e-06
F32 = jnp.float32
BF16 = jnp.bfloat16
LANES = 128
NB = 32
ANY = pl.BlockSpec(memory_space=pl.ANY)
VM = pl.BlockSpec(memory_space=pltpu.VMEM)
MESH = pl.DeviceIdType.MESH


def dct_np(length):
    freq = np.arange(length)[:, None]
    cells = np.arange(length)[None, :]
    scale = np.where(freq == 0, np.sqrt(1.0 / length), np.sqrt(2.0 / length))
    return scale * np.cos(np.pi * (cells + 0.5) * freq / length)


def eigen_np(length):
    return 4.0 * np.sin(np.pi * np.arange(length) / (2 * length)) ** 2


def hi_lo_np(table):
    kind = np.dtype(BF16)
    hi = table.astype(np.float32).astype(kind)
    lo = (table - hi.astype(np.float64)).astype(np.float32).astype(kind)
    return jnp.asarray(hi), jnp.asarray(lo)


def level_tables(rows):
    base = dct_np(NZ)
    size = NZ // rows
    groups = [base[g * size : (g + 1) * size] for g in range(rows)]
    fwd = np.stack([np.concatenate([groups[(r + s) % rows] for s in range(rows)], 0) for r in range(rows)])
    inv = np.stack([np.concatenate([groups[(r - s) % rows] for s in range(rows)], 0).T for r in range(rows)])
    return hi_lo_np(fwd), hi_lo_np(inv)


def split(x):
    hi = x.astype(BF16)
    lo = (x - hi.astype(F32)).astype(BF16)
    return hi, lo


def dot3(a_hi, a_lo, b_hi, b_lo):
    dot = functools.partial(jnp.dot, preferred_element_type=F32)
    return dot(a_hi, b_hi) + (dot(a_hi, b_lo) + dot(a_lo, b_hi))


def dot_nt(a, b):
    return lax.dot_general(a, b, (((1,), (1,)), ((), ())), preferred_element_type=F32)


def level_ids(shape=(NZ, LANES)):
    return lax.broadcasted_iota(jnp.int32, shape, 0)


def above(x):
    return pltpu.roll(x, NZ - 1, 0)


def below(x):
    return pltpu.roll(x, 1, 0)


def dz(x, ids):
    up = jnp.where(ids == NZ - 1, 0.0, above(x))
    down = jnp.where(ids == 0, 0.0, below(x))
    return 0.5 * (up - down)


def depth_of(ocean, depth):
    return jnp.where(ocean == 1, depth, 0)


def pack_kernel(f_ref, ocean_ref, depth_ref, ft_ref, p_ref, lo_ref, hi_ref):
    f = pl.program_id(0)
    ids = level_ids()
    lane = lax.broadcasted_iota(jnp.int32, (NZ, LANES), 1)
    depth = depth_of(ocean_ref[...], depth_ref[...])

    def slot_mask(lanes, slot):
        rel = lax.rem(lanes - 8 * slot + 3 + LANES, LANES)
        return rel < 6

    for g in range(NB // 16):
        packed = jnp.zeros((NZ, LANES), F32)
        packed_d = jnp.zeros((8, LANES), F32)
        lane8 = lax.broadcasted_iota(jnp.int32, (8, LANES), 1)
        for yi in range(16):
            y = g * 16 + yi
            row = depth[y : y + 1, :]
            q = jnp.where(ids < row, f_ref[0, pl.ds(y, NZ, stride=NB), :], 0.0)
            ft_ref[0, y] = q
            moved = pltpu.roll(q, 8 * yi, 1) if yi else q
            packed = jnp.where(slot_mask(lane, yi), moved, packed)
            d8 = jnp.broadcast_to(row.astype(F32), (8, LANES))
            moved_d = pltpu.roll(d8, 8 * yi, 1) if yi else d8
            packed_d = jnp.where(slot_mask(lane8, yi), moved_d, packed_d)
            if y < 3:
                lo_ref[pl.ds(pl.multiple_of((f * 3 + y) * NZ, NZ), NZ), :] = q
            if y >= NB - 3:
                hi_ref[pl.ds(pl.multiple_of((f * 3 + y - (NB - 3)) * NZ, NZ), NZ), :] = q
        p_ref[pl.ds(pl.multiple_of((f * 2 + g) * NZ, NZ), NZ), :] = packed
        p_ref[pl.ds(640 + g * 8, 8), :] = packed_d
    lo_ref[pl.ds(960, 8), :] = jnp.broadcast_to(depth[0:1].astype(F32), (8, LANES))
    hi_ref[pl.ds(960, 8), :] = jnp.broadcast_to(depth[NB - 1 : NB].astype(F32), (8, LANES))


def pack(fields, ocean, depth):
    full = lambda shape: pl.BlockSpec(shape, lambda f: (0,) * len(shape))
    return pl.pallas_call(
        pack_kernel,
        grid=(5,),
        in_specs=[
            pl.BlockSpec((1, NZ * NB, LANES), lambda f: (f, 0, 0)),
            full((NB, LANES)),
            full((NB, LANES)),
        ],
        out_specs=[
            pl.BlockSpec((1, NB, NZ, LANES), lambda f: (f, 0, 0, 0)),
            full((656, LANES)),
            full((968, LANES)),
            full((968, LANES)),
        ],
        out_shape=[
            jax.ShapeDtypeStruct((5, NB, NZ, LANES), F32),
            jax.ShapeDtypeStruct((656, LANES), F32),
            jax.ShapeDtypeStruct((968, LANES), F32),
            jax.ShapeDtypeStruct((968, LANES), F32),
        ],
        cost_estimate=pl.CostEstimate(flops=10_000_000, bytes_accessed=12_000_000, transcendentals=0),
        name="pack",
    )(fields.reshape(5, NZ * NB, LANES), ocean, depth)


def adjoint_kernel(rows, c_ref, ocean_ref, depth_ref, fh_ref, fl_ref, *outs):
    src = outs[rows]
    r = lax.axis_index("rows")
    ids = level_ids()
    depth = depth_of(ocean_ref[...], depth_ref[...])
    for half in range(4):
        for yi in range(8):
            y = half * 8 + yi
            w = jnp.where(ids < depth[y : y + 1, :], c_ref[0, pl.ds(y, NZ, stride=NB), :], 0.0)
            src[:, yi * LANES : (yi + 1) * LANES] = TIME_STEP * dz(w, ids)
        hi, lo = split(src[...])
        res = dot3(fh_ref[r], fl_ref[r], hi, lo)
        size = NZ // rows
        for s in range(rows):
            for yi in range(8):
                outs[s][half * 8 + yi] = res[s * size : (s + 1) * size, yi * LANES : (yi + 1) * LANES]


def adjoint_source(cotangent, ocean, depth, fwd, rows):
    size = NZ // rows
    return pl.pallas_call(
        functools.partial(adjoint_kernel, rows),
        grid=(1,),
        in_specs=[
            pl.BlockSpec((1, NZ * NB, LANES), lambda i: (2, 0, 0)),
            pl.BlockSpec((NB, LANES), lambda i: (0, 0)),
            pl.BlockSpec((NB, LANES), lambda i: (0, 0)),
            pl.BlockSpec((rows, NZ, NZ), lambda i: (0, 0, 0)),
            pl.BlockSpec((rows, NZ, NZ), lambda i: (0, 0, 0)),
        ],
        out_specs=[pl.BlockSpec((NB, size, LANES), lambda i: (0, 0, 0))] * rows,
        out_shape=[jax.ShapeDtypeStruct((NB, size, LANES), F32)] * rows,
        scratch_shapes=[pltpu.VMEM((NZ, 8 * LANES), F32)],
        cost_estimate=pl.CostEstimate(flops=10_000_000, bytes_accessed=2_100_000, transcendentals=0),
        name="adjoint",
    )(cotangent.reshape(5, NZ * NB, LANES), ocean, depth, *fwd)


def corrected(pos, speed, mag, y1, y2, y3, y4, y5, qm, qp):
    x1 = jnp.where(pos, y1, y5)
    x2 = jnp.where(pos, y2, y4)
    x3 = y3
    x4 = jnp.where(pos, y4, y2)
    c = jnp.where(pos, qm, qp)
    d1 = x2 - x1
    d2 = x3 - x2
    d3 = x4 - x3
    x3d = x3 + x3
    t0 = d1 + (x2 + x2)
    t1 = x2 + x3
    t2 = d3 - x3d
    eps4 = 4.0 * WENO_EPS
    e0 = (eps4 + t0 * t0) + (13.0 / 3.0) * (d1 * d1)
    e1 = (eps4 + t1 * t1) + (13.0 / 3.0) * (d2 * d2)
    e2 = (eps4 + t2 * t2) + (13.0 / 3.0) * (d3 * d3)
    f0 = e1 * e2
    f1 = e0 * e2
    f2 = e0 * e1
    g0 = f0 * f0
    g1 = 6.0 * (f1 * f1)
    g2 = 3.0 * (f2 * f2)
    k0 = t0 + d1 + x2
    k1 = t1 + x3
    k2 = x3d - d3 + x3
    num = g0 * k0 + g1 * k1 + g2 * k2
    den = g0 + g1 + g2
    return speed * c + mag * (num / den)


def advect_kernel(ft_ref, own_ref, east_ref, west_ref, south_ref, north_ref, depth_ref, ocean_ref,
                  adv_ref, spread_ref, ext, dext, exy, fxe, edge_d):
    zb = pl.program_id(0)
    z0 = pl.multiple_of(zb * 8, 8)
    zf = (lax.broadcasted_iota(jnp.int32, (8, LANES), 0) + z0).astype(F32)
    lane = lax.broadcasted_iota(jnp.int32, (8, LANES), 1)
    in_hi = lax.rem(lane, 8) < 4
    first, second = lane == 0, lane <= 1
    last, last2 = lane == LANES - 1, lane >= LANES - 2

    depth = depth_of(ocean_ref[...], depth_ref[...]).astype(F32)
    dext[8:40] = depth
    dext[7:8] = south_ref[960:961]
    dext[40:41] = north_ref[960:961]
    for f in range(5):
        for r in range(3):
            at = pl.ds(pl.multiple_of((f * 3 + r) * NZ + z0, 8), 8)
            ext[f, r] = south_ref[at]
            ext[f, 3 + NB + r] = north_ref[at]
        ext[f, 3 : 3 + NB] = ft_ref[f]

    for g in range(2):
        at_d = pl.ds(640 + g * 8, 8)
        edge_d[g] = jnp.where(in_hi, east_ref[at_d], west_ref[at_d])
        d_face = jnp.where(in_hi, east_ref[at_d], own_ref[at_d])
        d_face = jnp.minimum(d_face, pltpu.roll(d_face, 1, 1))
        for f in range(5):
            at = pl.ds(pl.multiple_of((f * 2 + g) * NZ + z0, 8), 8)
            exy[f, g] = jnp.where(in_hi, east_ref[at], west_ref[at])
            q = jnp.where(in_hi, east_ref[at], own_ref[at])
            qm = pltpu.roll(q, 1, 1)
            if f == 0:
                speed = jnp.where(zf < d_face, 0.5 * (q + qm), 0.0)
                pos = speed > 0
                mag = jnp.abs(speed) * (1.0 / 6.0)
            d = q - qm
            fxe[f, g] = corrected(
                pos, speed, mag, pltpu.roll(d, 2, 1), pltpu.roll(d, 1, 1), d,
                pltpu.roll(d, LANES - 1, 1), pltpu.roll(d, LANES - 2, 1), qm, q,
            )

    def face_y(j):
        d_face = jnp.minimum(dext[pl.ds(j + 7, 1), :], dext[pl.ds(j + 8, 1), :])
        out = []
        v = [ext[1, j + 2], ext[1, j + 3]]
        speed = jnp.where(zf < d_face, 0.5 * (v[0] + v[1]), 0.0)
        pos = speed > 0
        mag = jnp.abs(speed) * (1.0 / 6.0)
        dv = None
        for f in range(5):
            q = [ext[f, j + o] for o in range(6)]
            d = [q[o + 1] - q[o] for o in range(5)]
            if f == 1:
                dv = d[2]
            out.append(corrected(pos, speed, mag, d[0], d[1], d[2], d[3], d[4], q[2], q[3]))
        return out, dv

    def step(j, carry):
        below_flux, below_dv = carry
        above_flux, above_dv = face_y(j + 1)
        g = j // 16
        yi = lax.rem(j, 16)
        back = lax.rem(LANES - 8 * yi, LANES)
        to_last = LANES - 1 - 8 * yi
        drow = dext[pl.ds(j + 8, 1), :]
        d8 = jnp.broadcast_to(drow, (8, LANES))
        ed = pltpu.roll(edge_d[g], back, 1)
        d_face = jnp.minimum(d8, pltpu.roll(jnp.where(last, ed, d8), 1, 1))
        wet = zf < d8
        du = None
        for f in range(5):
            q = ext[f, j + 3]
            e = pltpu.roll(exy[f, g], back, 1)
            qm = pltpu.roll(jnp.where(last, e, q), 1, 1)
            em = pltpu.roll(jnp.where(last, q, e), 1, 1)
            d = q - qm
            de = e - em
            if f == 0:
                speed = jnp.where(zf < d_face, 0.5 * (q + qm), 0.0)
                pos = speed > 0
                mag = jnp.abs(speed) * (1.0 / 6.0)
            y1 = pltpu.roll(jnp.where(last2, de, d), 2, 1)
            y2 = pltpu.roll(jnp.where(last, de, d), 1, 1)
            y4 = pltpu.roll(jnp.where(first, de, d), LANES - 1, 1)
            y5 = pltpu.roll(jnp.where(second, de, d), LANES - 2, 1)
            if f == 0:
                du = d + y4
            flux = corrected(pos, speed, mag, y1, y2, d, y4, y5, qm, q)
            east = jnp.where(last, pltpu.roll(fxe[f, g], to_last, 1), pltpu.roll(flux, LANES - 1, 1))
            total = (flux - east) + (below_flux[f] - above_flux[f])
            adv_ref[f, j] = jnp.where(wet, q + TIME_STEP * total, 0.0)
        spread_ref[j] = 0.5 * du + 0.5 * (below_dv + above_dv)
        return above_flux, above_dv

    lax.fori_loop(0, NB, step, face_y(0))


def advect(ft, own, east, west, south, north, depth, ocean):
    full = lambda shape: pl.BlockSpec(shape, lambda i: (0,) * len(shape))
    return pl.pallas_call(
        advect_kernel,
        grid=(NZ // 8,),
        in_specs=[
            pl.BlockSpec((5, NB, 8, LANES), lambda i: (0, 0, i, 0)),
            full((656, LANES)), full((656, LANES)), full((656, LANES)),
            full((968, LANES)), full((968, LANES)),
            full((NB, LANES)), full((NB, LANES)),
        ],
        out_specs=[
            pl.BlockSpec((5, NB, 8, LANES), lambda i: (0, 0, i, 0)),
            pl.BlockSpec((NB, 8, LANES), lambda i: (0, i, 0)),
        ],
        out_shape=[
            jax.ShapeDtypeStruct((5, NB, NZ, LANES), F32),
            jax.ShapeDtypeStruct((NB, NZ, LANES), F32),
        ],
        scratch_shapes=[
            pltpu.VMEM((5, NB + 6, 8, LANES), F32),
            pltpu.VMEM((48, LANES), F32),
            pltpu.VMEM((5, 2, 8, LANES), F32),
            pltpu.VMEM((5, 2, 8, LANES), F32),
            pltpu.VMEM((2, 8, LANES), F32),
        ],
        cost_estimate=pl.CostEstimate(flops=200_000_000, bytes_accessed=130_000_000, transcendentals=0),
        name="advect",
    )(ft, own, east, west, south, north, depth, ocean)


def forward_kernel(rows, adv_ref, w_ref, spread_ref, depth_ref, ocean_ref, win_ref, bin_ref, wout_ref,
                   fh_ref, fl_ref, *refs):
    pieces = refs[:rows]
    rates_ref, act_ref, hs_ref, feats, rate_s, src = refs[rows:]
    r = lax.axis_index("rows")
    ids = level_ids()
    depth = depth_of(ocean_ref[...], depth_ref[...])
    for n, f in enumerate((0, 1, 3, 4)):
        for yi in range(8):
            feats[n * NZ : (n + 1) * NZ, yi * LANES : (yi + 1) * LANES] = adv_ref[f, yi].astype(BF16)
    pre = lax.dot_general(win_ref[...], feats[...], (((0,), (0,)), ((), ())), preferred_element_type=F32)
    act = jnp.tanh(pre + bin_ref[...])
    act_ref[0] = act
    out = lax.dot_general(wout_ref[...], act.astype(BF16), (((0,), (0,)), ((), ())), preferred_element_type=F32)
    rate_s[...] = 2.0 * jax.nn.sigmoid(out)
    for yi in range(8):
        cols = slice(yi * LANES, (yi + 1) * LANES)
        row = depth[yi : yi + 1, :]
        wet = ids < row
        rates = rate_s[:, cols]
        rates_ref[yi] = rates
        mixed = []
        for n, f in enumerate((3, 4)):
            t = adv_ref[f, yi]
            flux = jnp.where(ids + 1 < row, rates * (above(t) - t), 0.0)
            m = jnp.where(wet, t + TIME_STEP * (flux - below(flux)), 0.0)
            hs_ref[n, yi] = m
            mixed.append(m)
        density = 0.5 * mixed[0] - 0.5 * mixed[1]
        rhs = dz(density, ids) - (spread_ref[yi] + dz(w_ref[0, yi], ids)) / TIME_STEP
        src[:, cols] = jnp.where(wet, rhs, 0.0)
    hi, lo = split(src[...])
    res = dot3(fh_ref[r], fl_ref[r], hi, lo)
    size = NZ // rows
    for s in range(rows):
        for yi in range(8):
            pieces[s][yi] = res[s * size : (s + 1) * size, yi * LANES : (yi + 1) * LANES]


def closure_forward(adv, ft, spread, depth, ocean, win, b_in, wout, fwd, rows):
    size = NZ // rows
    full = lambda shape: pl.BlockSpec(shape, lambda i: (0,) * len(shape))
    plane = pl.BlockSpec((8, LANES), lambda i: (i, 0))
    ycol = pl.BlockSpec((8, NZ, LANES), lambda i: (i, 0, 0))
    return pl.pallas_call(
        functools.partial(forward_kernel, rows),
        grid=(NB // 8,),
        in_specs=[
            pl.BlockSpec((5, 8, NZ, LANES), lambda i: (0, i, 0, 0)),
            pl.BlockSpec((1, 8, NZ, LANES), lambda i: (2, i, 0, 0)),
            ycol, plane, plane,
            full((256, 256)), full((256, 1)), full((256, NZ)),
            full((rows, NZ, NZ)), full((rows, NZ, NZ)),
        ],
        out_specs=[pl.BlockSpec((8, size, LANES), lambda i: (i, 0, 0))] * rows
        + [ycol, pl.BlockSpec((1, 256, 1024), lambda i: (i, 0, 0)),
           pl.BlockSpec((2, 8, NZ, LANES), lambda i: (0, i, 0, 0))],
        out_shape=[jax.ShapeDtypeStruct((NB, size, LANES), F32)] * rows
        + [
            jax.ShapeDtypeStruct((NB, NZ, LANES), F32),
            jax.ShapeDtypeStruct((NB // 8, 256, 1024), F32),
            jax.ShapeDtypeStruct((2, NB, NZ, LANES), F32),
        ],
        scratch_shapes=[
            pltpu.VMEM((256, 1024), BF16),
            pltpu.VMEM((NZ, 1024), F32),
            pltpu.VMEM((NZ, 1024), F32),
        ],
        cost_estimate=pl.CostEstimate(flops=900_000_000, bytes_accessed=18_000_000, transcendentals=1_500_000),
        name="closure_forward",
    )(adv, ft, spread, depth, ocean, win, b_in, wout, *fwd)


def root_of(d):
    q = jnp.sqrt(d + 0.25 * d * d)
    return 1.0 / (1.0 + 0.5 * d + q), 0.5 / q


def exchange_rows(rows, cols, chunk):
    n = NZ // cols
    tile = max(8, 2 * n)
    start = (chunk // n) * tile + chunk % n
    return start, (rows // n) * tile, n, tile


def line_kernel(rows, cols, *refs):
    pieces = refs[:rows]
    ch_ref, cl_ref, lv_ref, ex_ref, v_ref, s_ref, work = refs[rows:]
    r = lax.axis_index("rows")
    size = NZ // rows
    wide = rows * LANES
    total = None
    for s in range(rows):
        src = lax.rem(r - s + rows, rows)
        at = pl.ds(pl.multiple_of(src * LANES, LANES), LANES)
        hi, lo = split(pieces[s][...])
        part = dot3(hi, lo, ch_ref[at, :], cl_ref[at, :])
        total = part if total is None else total + part
    work[...] = total
    d = lv_ref[pl.ds(pl.multiple_of(r * size, size), size), :] + ex_ref[...]
    lam, _ = root_of(d)

    def causal(y, c):
        at = pl.ds(pl.multiple_of(y * size, size), size)
        c = work[at] + lam * c
        v_ref[at] = c
        return c

    end = lax.fori_loop(0, NB, causal, jnp.zeros((size, wide), F32))

    def anticausal(i, a):
        at = pl.ds(pl.multiple_of((NB - 1 - i) * size, size), size)
        x = work[at]
        v_ref[at] = v_ref[at] + lam * a
        return x + lam * a

    start = lax.fori_loop(0, NB, anticausal, jnp.zeros((size, wide), F32))
    s_ref[...] = jnp.zeros_like(s_ref)
    for ch in range(rows):
        row, stride, n, _ = exchange_rows(rows, cols, ch)
        lanes = slice(ch * LANES, (ch + 1) * LANES)
        s_ref[pl.ds(row, size, stride=stride), :] = start[:, lanes]
        s_ref[pl.ds(row + n, size, stride=stride), :] = end[:, lanes]


def line_solve(pieces, tables, rows, cols):
    size = NZ // rows
    wide = rows * LANES
    tile = exchange_rows(rows, cols, 0)[3]
    return pl.pallas_call(
        functools.partial(line_kernel, rows, cols),
        in_specs=[VM] * (rows + 4),
        out_specs=[VM, VM],
        out_shape=[
            jax.ShapeDtypeStruct((NB * size, wide), F32),
            jax.ShapeDtypeStruct((cols * tile, LANES), F32),
        ],
        scratch_shapes=[pltpu.VMEM((NB * size, wide), F32)],
        cost_estimate=pl.CostEstimate(flops=800_000_000, bytes_accessed=4_500_000, transcendentals=0),
        name="line_solve",
    )(*[p.reshape(NB * size, LANES) for p in pieces], *tables)


def carry_kernel(rows, cols, s_ref, lv_ref, ex_ref, c_ref, got, send, dsem, send_sem, recv_sem, send2_sem, recv2_sem):
    n = NZ // cols
    tile = max(8, 2 * n)
    me = lax.axis_index("cols")
    r = lax.axis_index("rows")
    barrier = pltpu.get_barrier_semaphore()

    def greet(t, carry):
        pl.semaphore_signal(barrier, inc=1, device_id={"cols": lax.rem(me + t, cols)}, device_id_type=MESH)
        return carry

    lax.fori_loop(1, cols, greet, 0)
    pl.semaphore_wait(barrier, cols - 1)

    def out_copy(t):
        peer = lax.rem(me + t, cols)
        return pltpu.make_async_remote_copy(
            src_ref=s_ref.at[peer], dst_ref=got.at[me], send_sem=send_sem.at[t], recv_sem=recv_sem.at[t],
            device_id={"cols": peer}, device_id_type=MESH,
        )

    def back_copy(t):
        peer = lax.rem(me + t, cols)
        return pltpu.make_async_remote_copy(
            src_ref=send.at[peer], dst_ref=c_ref.at[me], send_sem=send2_sem.at[t], recv_sem=recv2_sem.at[t],
            device_id={"cols": peer}, device_id_type=MESH,
        )

    def run(make):
        lax.fori_loop(1, cols, lambda t, c: (make(t).start(), c)[1], 0)

    def finish(make):
        lax.fori_loop(1, cols, lambda t, c: (make(t).wait(), c)[1], 0)

    run(out_copy)
    mine = pltpu.make_async_copy(s_ref.at[me], got.at[me], dsem.at[0])
    mine.start()
    size = NZ // rows
    level = r * size + (me * n) // rows
    chunk = lax.rem(me, rows // n)
    lam, _ = root_of(lv_ref[level] + ex_ref[chunk])
    mu = lam
    for _ in range(NB.bit_length() - 1):
        mu = mu * mu
    whole = mu
    for _ in range(cols.bit_length() - 1):
        whole = whole * whole
    scale = 1.0 / (1.0 - whole * whole)
    is_start = lax.broadcasted_iota(jnp.int32, (tile, LANES), 0) < n
    mine.wait()
    finish(out_copy)

    zero = jnp.zeros((tile, LANES), F32)
    sa = lax.fori_loop(0, cols, lambda k, a: got[cols - 1 - k] + mu * a, zero)
    sb = lax.fori_loop(0, cols, lambda k, b: got[k] + mu * b, zero)
    left = (pltpu.roll(sa, n, 0) + whole * sb) * scale
    right = (pltpu.roll(sb, tile - n, 0) + whole * sa) * scale

    def ascend(k, c):
        send[k] = c
        return got[k] + mu * c

    lax.fori_loop(0, cols, ascend, left)

    def descend(i, c):
        k = cols - 1 - i
        send[k] = jnp.where(is_start, c, send[k])
        return got[k] + mu * c

    lax.fori_loop(0, cols, descend, right)
    run(back_copy)
    mine2 = pltpu.make_async_copy(send.at[me], c_ref.at[me], dsem.at[1])
    mine2.start()
    mine2.wait()
    finish(back_copy)


def carries(moments, rows, cols, cid):
    _, _, n, tile = exchange_rows(rows, cols, 0)
    level_list = jnp.asarray(SPECTRAL_SHIFT + eigen_np(NZ), F32)
    east = eigen_np(rows * LANES).reshape(rows // n, n, LANES)
    east_tiles = jnp.asarray(east[:, np.arange(tile) % n], F32)
    return pl.pallas_call(
        functools.partial(carry_kernel, rows, cols),
        in_specs=[VM, pl.BlockSpec(memory_space=pltpu.SMEM), VM],
        out_specs=VM,
        out_shape=jax.ShapeDtypeStruct((cols, tile, LANES), F32),
        scratch_shapes=[
            pltpu.VMEM((cols, tile, LANES), F32),
            pltpu.VMEM((cols, tile, LANES), F32),
            pltpu.SemaphoreType.DMA((2,)),
            pltpu.SemaphoreType.DMA((cols,)),
            pltpu.SemaphoreType.DMA((cols,)),
            pltpu.SemaphoreType.DMA((cols,)),
            pltpu.SemaphoreType.DMA((cols,)),
        ],
        compiler_params=pltpu.CompilerParams(collective_id=cid, has_side_effects=True),
        name="carries",
    )(moments.reshape(cols, tile, LANES), level_list, east_tiles)


def back_kernel(rows, cols, v_ref, c_ref, ch_ref, cl_ref, lv_ref, ex_ref, *refs):
    outs = refs[:rows]
    work = refs[rows]
    r = lax.axis_index("rows")
    size = NZ // rows
    d = lv_ref[pl.ds(pl.multiple_of(r * size, size), size), :] + ex_ref[...]
    lam, kappa = root_of(d)
    left, right = [], []
    for ch in range(rows):
        row, stride, n, _ = exchange_rows(rows, cols, ch)
        right.append(c_ref[pl.ds(row, size, stride=stride), :])
        left.append(c_ref[pl.ds(row + n, size, stride=stride), :])
    left = jnp.concatenate(left, 1) * (lam * kappa)
    right = jnp.concatenate(right, 1) * (lam * kappa)

    def fwd(y, h):
        at = pl.ds(pl.multiple_of(y * size, size), size)
        work[at] = kappa * v_ref[at] + h
        return lam * h

    lax.fori_loop(0, NB, fwd, left)

    def bwd(i, h):
        at = pl.ds(pl.multiple_of((NB - 1 - i) * size, size), size)
        work[at] = work[at] + h
        return lam * h

    lax.fori_loop(0, NB, bwd, right)
    hi, lo = split(work[...])
    for s in range(rows):
        dst = lax.rem(r + s, rows)
        outs[s][...] = dot3(hi, lo, ch_ref[dst], cl_ref[dst])


def line_back(v, c, tables, rows, cols):
    size = NZ // rows
    outs = pl.pallas_call(
        functools.partial(back_kernel, rows, cols),
        in_specs=[VM] * 6,
        out_specs=[VM] * rows,
        out_shape=[jax.ShapeDtypeStruct((NB * size, LANES), F32)] * rows,
        scratch_shapes=[pltpu.VMEM((NB * size, rows * LANES), F32)],
        cost_estimate=pl.CostEstimate(flops=800_000_000, bytes_accessed=4_500_000, transcendentals=0),
        name="line_back",
    )(v, c.reshape(-1, LANES), *tables)
    return [o.reshape(NB, size, LANES) for o in outs]


def gather_levels(pieces, rows, buf, base=0):
    size = NZ // rows
    for s in range(rows):
        for yi in range(8):
            buf[s * size : (s + 1) * size, yi * LANES : (yi + 1) * LANES] = pieces[s][base + yi]


def backward_kernel(rows, *refs):
    pieces = refs[:rows]
    (adv_ref, ct_ref, cs_ref, rates_ref, act_ref, depth_ref, ocean_ref, wout_ref, ih_ref, il_ref,
     g_ref, buf, feats, gos, gw, gwo, gb) = refs[rows:]
    i = pl.program_id(0)
    r = lax.axis_index("rows")
    ids = level_ids()
    depth = depth_of(ocean_ref[...], depth_ref[...])
    gather_levels(pieces, rows, buf)
    hi, lo = split(buf[...])
    buf[...] = dot3(ih_ref[r], il_ref[r], hi, lo)
    for n, f in enumerate((0, 1, 3, 4)):
        for yi in range(8):
            feats[n * NZ : (n + 1) * NZ, yi * LANES : (yi + 1) * LANES] = adv_ref[f, yi].astype(BF16)
    for yi in range(8):
        cols = slice(yi * LANES, (yi + 1) * LANES)
        row = depth[yi : yi + 1, :]
        wet = ids < row
        grad_density = -dz(jnp.where(wet, buf[:, cols], 0.0), ids)
        rates = rates_ref[yi]
        total = None
        for f, c_ref, sign in ((3, ct_ref, 0.5), (4, cs_ref, -0.5)):
            grad = c_ref[0, pl.ds(yi, NZ, stride=8), :] + sign * grad_density
            grad = jnp.where(wet, grad, 0.0)
            t = adv_ref[f, yi]
            term = (grad - above(grad)) * (above(t) - t)
            total = term if total is None else total + term
        grad_rates = jnp.where(ids + 1 < row, TIME_STEP * total, 0.0)
        gos[:, cols] = (grad_rates * rates * (1.0 - 0.5 * rates)).astype(BF16)
    act = act_ref[0]
    go = gos[...]
    gpre = jnp.dot(wout_ref[...], go, preferred_element_type=F32) * (1.0 - act * act)
    p_hi, p_lo = split(gpre)
    ones = jnp.ones((8, 1024), BF16)

    @pl.when(i == 0)
    def _():
        gw[...] = jnp.zeros_like(gw)
        gwo[...] = jnp.zeros_like(gwo)
        gb[...] = jnp.zeros_like(gb)

    gw[...] += dot_nt(feats[...], p_hi)
    gwo[...] += dot_nt(go, act.astype(BF16))
    gb[...] += dot_nt(ones, p_hi) + dot_nt(ones, p_lo)

    @pl.when(i == NB // 8 - 1)
    def _():
        for h in range(2):
            lanes = slice(h * LANES, (h + 1) * LANES)
            g_ref[h * 256 : (h + 1) * 256] = gw[:, lanes]
            g_ref[512 + h * NZ : 512 + (h + 1) * NZ] = gwo[:, lanes]
            g_ref[575 + h * NZ : 576 + h * NZ] = gb[0:1, lanes]
        g_ref[640:1024] = jnp.zeros((384, LANES), F32)


def closure_backward(pieces, adv, cotangent, rates, act, depth, ocean, wout, inv, rows):
    size = NZ // rows
    full = lambda shape: pl.BlockSpec(shape, lambda i: (0,) * len(shape))
    plane = pl.BlockSpec((8, LANES), lambda i: (i, 0))
    ycol = pl.BlockSpec((8, NZ, LANES), lambda i: (i, 0, 0))
    cot = cotangent.reshape(5, NZ, NB // 8, 8, LANES)

    def kernel(*refs):
        refs = list(refs)
        for at in (rows + 1, rows + 2):
            refs[at] = refs[at].reshape(1, NZ * 8, LANES)
        backward_kernel(rows, *refs)

    cot_spec = lambda f: pl.BlockSpec((1, NZ, 1, 8, LANES), lambda i: (f, 0, i, 0, 0))
    return pl.pallas_call(
        kernel,
        grid=(NB // 8,),
        in_specs=[pl.BlockSpec((8, size, LANES), lambda i: (i, 0, 0))] * rows
        + [
            pl.BlockSpec((5, 8, NZ, LANES), lambda i: (0, i, 0, 0)),
            cot_spec(3), cot_spec(4), ycol,
            pl.BlockSpec((1, 256, 1024), lambda i: (i, 0, 0)),
            plane, plane, full((256, NZ)), full((rows, NZ, NZ)), full((rows, NZ, NZ)),
        ],
        out_specs=full((1024, LANES)),
        out_shape=jax.ShapeDtypeStruct((1024, LANES), F32),
        scratch_shapes=[
            pltpu.VMEM((NZ, 1024), F32),
            pltpu.VMEM((256, 1024), BF16),
            pltpu.VMEM((NZ, 1024), BF16),
            pltpu.VMEM((256, 256), F32),
            pltpu.VMEM((NZ, 256), F32),
            pltpu.VMEM((8, 256), F32),
        ],
        cost_estimate=pl.CostEstimate(flops=1_200_000_000, bytes_accessed=16_000_000, transcendentals=0),
        name="closure_backward",
    )(*pieces, adv, cot, cot, rates, act, depth, ocean, wout, *inv)


def sum_kernel(rows, cols, g_ref, o_ref, land, acc, land2, total, dsem, s1, r1, s2, r2, s3, r3, s4, r4):
    me = lax.axis_index("cols")
    r = lax.axis_index("rows")
    barrier = pltpu.get_barrier_semaphore()

    def greet(t, carry):
        pl.semaphore_signal(barrier, inc=1, device_id={"cols": lax.rem(me + t, cols)}, device_id_type=MESH)
        return carry

    lax.fori_loop(1, cols, greet, 0)
    for t in range(1, rows):
        pl.semaphore_signal(barrier, inc=1, device_id={"rows": lax.rem(r + t, rows)}, device_id_type=MESH)
    pl.semaphore_wait(barrier, cols - 1 + rows - 1)

    def copy(axis, count, at, t, src, dst, ss, rs):
        return pltpu.make_async_remote_copy(
            src_ref=src, dst_ref=dst, send_sem=ss.at[t], recv_sem=rs.at[t],
            device_id={axis: lax.rem(at + t, count)}, device_id_type=MESH,
        )

    def rows_out(t):
        return copy("rows", rows, r, t, g_ref.at[lax.rem(r + t, rows)], land.at[t], s1, r1)

    def cols_out(t):
        return copy("cols", cols, me, t, acc.at[lax.rem(me + t, cols)], land2.at[t], s2, r2)

    def cols_back(t):
        return copy("cols", cols, me, t, total.at[me], total.at[me], s3, r3)

    def rows_back(t):
        return copy("rows", rows, r, t, total, o_ref.at[r], s4, r4)

    def all_of(make, count):
        lax.fori_loop(1, count, lambda t, c: (make(t).start(), c)[1], 0)
        lax.fori_loop(1, count, lambda t, c: (make(t).wait(), c)[1], 0)

    all_of(rows_out, rows)
    value = g_ref[r]
    for t in range(1, rows):
        value = value + land[t]
    acc[...] = value
    all_of(cols_out, cols)
    tile = lax.fori_loop(1, cols, lambda t, v: v + land2[t], acc[me])
    total[me] = tile
    all_of(cols_back, cols)
    own = pltpu.make_async_copy(total, o_ref.at[r], dsem.at[0])
    own.start()
    all_of(rows_back, rows)
    own.wait()


def sum_gradients(g, rows, cols, cid):
    tile = 1024 // (rows * cols)
    sems = []
    for count in (rows, cols, cols, rows):
        sems += [pltpu.SemaphoreType.DMA((count,)), pltpu.SemaphoreType.DMA((count,))]
    return pl.pallas_call(
        functools.partial(sum_kernel, rows, cols),
        in_specs=[VM],
        out_specs=VM,
        out_shape=jax.ShapeDtypeStruct((rows, cols, tile, LANES), F32),
        scratch_shapes=[
            pltpu.VMEM((rows, cols, tile, LANES), F32),
            pltpu.VMEM((cols, tile, LANES), F32),
            pltpu.VMEM((cols, tile, LANES), F32),
            pltpu.VMEM((cols, tile, LANES), F32),
            pltpu.SemaphoreType.DMA((1,)),
            *sems,
        ],
        compiler_params=pltpu.CompilerParams(collective_id=cid, has_side_effects=True),
        name="sum_gradients",
    )(g.reshape(rows, cols, tile, LANES)).reshape(1024, LANES)


def place_kernel(adv_ref, hs_ref, o_ref):
    i = pl.program_id(0)

    @pl.when(i < 2)
    def _():
        for y in range(NB):
            o_ref[0, pl.ds(y, NZ, stride=NB), :] = adv_ref[0, y]

    @pl.when(i >= 2)
    def _():
        for y in range(NB):
            o_ref[0, pl.ds(y, NZ, stride=NB), :] = hs_ref[0, y]


def place(adv, hs):
    block = lambda index: pl.BlockSpec((1, NB, NZ, LANES), index)
    return pl.pallas_call(
        place_kernel,
        grid=(4,),
        in_specs=[
            block(lambda i: (jnp.minimum(i, 1), 0, 0, 0)),
            block(lambda i: (jnp.maximum(i - 2, 0), 0, 0, 0)),
        ],
        out_specs=pl.BlockSpec((1, NZ * NB, LANES), lambda i: (i + (i >= 2), 0, 0)),
        out_shape=jax.ShapeDtypeStruct((5, NZ * NB, LANES), F32),
        cost_estimate=pl.CostEstimate(flops=1_000_000, bytes_accessed=8_400_000, transcendentals=0),
        name="place",
    )(adv, hs)


def finish_kernel(rows, *refs):
    pieces = refs[:rows]
    adv_ref, depth_ref, ocean_ref, ih_ref, il_ref, _, o_ref, p_ref, buf = refs[rows:]
    r = lax.axis_index("rows")
    ids = level_ids()
    depth = depth_of(ocean_ref[...], depth_ref[...])
    for part in range(NB // 8):
        gather_levels(pieces, rows, buf, part * 8)
        hi, lo = split(buf[...])
        pressure = dot3(ih_ref[r], il_ref[r], hi, lo)
        for yi in range(8):
            y = part * 8 + yi
            p = pressure[:, yi * LANES : (yi + 1) * LANES]
            p_ref[pl.ds(y, NZ, stride=NB), :] = p
            new_w = jnp.where(ids < depth[y : y + 1, :], adv_ref[0, y] - TIME_STEP * dz(p, ids), 0.0)
            o_ref[0, pl.ds(y, NZ, stride=NB), :] = new_w


def finish(pieces, adv, depth, ocean, inv, placed, rows):
    size = NZ // rows
    full = lambda shape: pl.BlockSpec(shape, lambda i: (0,) * len(shape))
    return pl.pallas_call(
        functools.partial(finish_kernel, rows),
        grid=(1,),
        in_specs=[full((NB, size, LANES))] * rows
        + [
            pl.BlockSpec((1, NB, NZ, LANES), lambda i: (2, 0, 0, 0)),
            full((NB, LANES)), full((NB, LANES)), full((rows, NZ, NZ)), full((rows, NZ, NZ)), ANY,
        ],
        out_specs=[pl.BlockSpec((1, NZ * NB, LANES), lambda i: (2, 0, 0)), full((NZ * NB, LANES))],
        out_shape=[
            jax.ShapeDtypeStruct((5, NZ * NB, LANES), F32),
            jax.ShapeDtypeStruct((NZ * NB, LANES), F32),
        ],
        scratch_shapes=[pltpu.VMEM((NZ, 1024), F32)],
        input_output_aliases={rows + 5: 0},
        cost_estimate=pl.CostEstimate(flops=50_000_000, bytes_accessed=4_200_000, transcendentals=0),
        name="finish",
    )(*pieces, adv, depth, ocean, *inv, placed)


def shift_pieces(pieces, rows):
    got = [pieces[0]]
    for s in range(1, rows):
        got.append(lax.ppermute(pieces[s], "rows", [(i, (i + s) % rows) for i in range(rows)]))
    return got


def per_device(rows, cols, fields, cotangent, ocean, depth, in_weight, in_bias, out_weight):
    fwd, inv = level_tables(rows)
    east_np = dct_np(rows * LANES)
    east_fwd = hi_lo_np(east_np.T)
    east_inv = hi_lo_np(np.stack(np.split(east_np, rows, axis=1)))
    levels = jnp.asarray(np.repeat((SPECTRAL_SHIFT + eigen_np(NZ))[:, None], rows * LANES, 1), F32)
    easts = jnp.asarray(eigen_np(rows * LANES)[None, :], F32)
    b_in = in_bias[:, None]
    wout = jnp.pad(out_weight, ((0, 0), (0, 1)))

    ft, own, lo, hi = pack(fields, ocean, depth)
    up_r = [(i, i + 1) for i in range(rows - 1)]
    up_c = [(i, i + 1) for i in range(cols - 1)]
    down_r = [(b, a) for a, b in up_r]
    down_c = [(b, a) for a, b in up_c]
    south = lax.ppermute(hi, "cols", up_c)
    north = lax.ppermute(lo, "cols", down_c)
    west = lax.ppermute(own, "rows", up_r)
    east = lax.ppermute(own, "rows", down_r)

    adj = shift_pieces(adjoint_source(cotangent, ocean, depth, fwd, rows), rows)
    adv, spread = advect(ft, own, east, west, south, north, depth, ocean)

    v, moments = line_solve(adj, (*east_fwd, levels, easts), rows, cols)
    c = carries(moments, rows, cols, 1)
    adj = shift_pieces(line_back(v, c, (*east_inv, levels, easts), rows, cols), rows)

    *pieces, rates, act, hs = closure_forward(adv, ft, spread, depth, ocean, in_weight, b_in, wout, fwd, rows)
    pieces = shift_pieces(pieces, rows)
    grads = closure_backward(adj, adv, cotangent, rates, act, depth, ocean, wout, inv, rows)
    placed = place(adv, hs)

    v, moments = line_solve(pieces, (*east_fwd, levels, easts), rows, cols)
    c = carries(moments, rows, cols, 1)
    pieces = shift_pieces(line_back(v, c, (*east_inv, levels, easts), rows, cols), rows)
    grads = sum_gradients(grads, rows, cols, 2)
    new_fields, pressure = finish(pieces, adv, depth, ocean, inv, placed, rows)

    g_in = jnp.concatenate([grads[0:256], grads[256:512]], 1)
    g_out = jnp.concatenate([grads[512:576], grads[576:640]], 1)
    return (
        new_fields.reshape(5, NZ, NB, LANES),
        pressure.reshape(NZ, NB, LANES),
        g_in,
        g_out[NZ - 1],
        g_out[: NZ - 1].T,
    )


def solution(mesh):
    rows, cols = mesh.shape["rows"], mesh.shape["cols"]
    in_specs = (
        P(None, None, "cols", "rows"),
        P(None, None, "cols", "rows"),
        P("cols", "rows"),
        P("cols", "rows"),
        P(),
        P(),
        P(),
    )
    out_specs = (P(None, None, "cols", "rows"), P(None, "cols", "rows"), P(), P(), P())
    return jax.shard_map(
        functools.partial(per_device, rows, cols),
        mesh=mesh, in_specs=in_specs, out_specs=out_specs, check_vma=False,
    )
```

```python
import functools
import math

import jax
import jax.numpy as jnp
import numpy as np
from jax import lax
from jax.experimental import pallas as pl
from jax.experimental.pallas import tpu as pltpu
from jax.sharding import PartitionSpec as P

NZ = 64
TIME_STEP = 0.2
SPECTRAL_SHIFT = 0.001
WENO_EPS = 1e-06
F32 = jnp.float32
BF16 = jnp.bfloat16
LANES = 128
NB = 32
ANY = pl.BlockSpec(memory_space=pl.ANY)
VM = pl.BlockSpec(memory_space=pltpu.VMEM)
MESH = pl.DeviceIdType.MESH


def dct_np(length):
    freq = np.arange(length)[:, None]
    cells = np.arange(length)[None, :]
    scale = np.where(freq == 0, np.sqrt(1.0 / length), np.sqrt(2.0 / length))
    return scale * np.cos(np.pi * (cells + 0.5) * freq / length)


def eigen_np(length):
    return 4.0 * np.sin(np.pi * np.arange(length) / (2 * length)) ** 2


def hi_lo_np(table):
    kind = np.dtype(BF16)
    hi = table.astype(np.float32).astype(kind)
    lo = (table - hi.astype(np.float64)).astype(np.float32).astype(kind)
    return jnp.asarray(hi), jnp.asarray(lo)


def level_tables(rows):
    base = dct_np(NZ)
    size = NZ // rows
    groups = [base[g * size : (g + 1) * size] for g in range(rows)]
    fwd = np.stack([np.concatenate([groups[(r + s) % rows] for s in range(rows)], 0) for r in range(rows)])
    inv = np.stack([np.concatenate([groups[(r - s) % rows] for s in range(rows)], 0).T for r in range(rows)])
    return hi_lo_np(fwd), hi_lo_np(inv)


def split(x):
    hi = x.astype(BF16)
    lo = (x - hi.astype(F32)).astype(BF16)
    return hi, lo


def dot3(a_hi, a_lo, b_hi, b_lo):
    dot = functools.partial(jnp.dot, preferred_element_type=F32)
    return dot(a_hi, b_hi) + (dot(a_hi, b_lo) + dot(a_lo, b_hi))


def dot_nt(a, b):
    return lax.dot_general(a, b, (((1,), (1,)), ((), ())), preferred_element_type=F32)


def level_ids(shape=(NZ, LANES)):
    return lax.broadcasted_iota(jnp.int32, shape, 0)


def above(x):
    return pltpu.roll(x, NZ - 1, 0)


def below(x):
    return pltpu.roll(x, 1, 0)


def dz(x, ids):
    up = jnp.where(ids == NZ - 1, 0.0, above(x))
    down = jnp.where(ids == 0, 0.0, below(x))
    return 0.5 * (up - down)


def depth_of(ocean, depth):
    return jnp.where(ocean == 1, depth, 0)


def pack_kernel(f_ref, ocean_ref, depth_ref, ft_ref, p_ref, lo_ref, hi_ref):
    f = pl.program_id(0)
    ids = level_ids()
    lane = lax.broadcasted_iota(jnp.int32, (NZ, LANES), 1)
    depth = depth_of(ocean_ref[...], depth_ref[...])

    def slot_mask(lanes, slot):
        rel = lax.rem(lanes - 8 * slot + 3 + LANES, LANES)
        return rel < 6

    for g in range(NB // 16):
        packed = jnp.zeros((NZ, LANES), F32)
        packed_d = jnp.zeros((8, LANES), F32)
        lane8 = lax.broadcasted_iota(jnp.int32, (8, LANES), 1)
        for yi in range(16):
            y = g * 16 + yi
            row = depth[y : y + 1, :]
            q = jnp.where(ids < row, f_ref[0, pl.ds(y, NZ, stride=NB), :], 0.0)
            ft_ref[0, y] = q
            moved = pltpu.roll(q, 8 * yi, 1) if yi else q
            packed = jnp.where(slot_mask(lane, yi), moved, packed)
            d8 = jnp.broadcast_to(row.astype(F32), (8, LANES))
            moved_d = pltpu.roll(d8, 8 * yi, 1) if yi else d8
            packed_d = jnp.where(slot_mask(lane8, yi), moved_d, packed_d)
            if y < 3:
                lo_ref[pl.ds(pl.multiple_of((f * 3 + y) * NZ, NZ), NZ), :] = q
            if y >= NB - 3:
                hi_ref[pl.ds(pl.multiple_of((f * 3 + y - (NB - 3)) * NZ, NZ), NZ), :] = q
        p_ref[pl.ds(pl.multiple_of((f * 2 + g) * NZ, NZ), NZ), :] = packed
        p_ref[pl.ds(640 + g * 8, 8), :] = packed_d
    lo_ref[pl.ds(960, 8), :] = jnp.broadcast_to(depth[0:1].astype(F32), (8, LANES))
    hi_ref[pl.ds(960, 8), :] = jnp.broadcast_to(depth[NB - 1 : NB].astype(F32), (8, LANES))


def pack(fields, ocean, depth):
    full = lambda shape: pl.BlockSpec(shape, lambda f: (0,) * len(shape))
    return pl.pallas_call(
        pack_kernel,
        grid=(5,),
        in_specs=[
            pl.BlockSpec((1, NZ * NB, LANES), lambda f: (f, 0, 0)),
            full((NB, LANES)),
            full((NB, LANES)),
        ],
        out_specs=[
            pl.BlockSpec((1, NB, NZ, LANES), lambda f: (f, 0, 0, 0)),
            full((656, LANES)),
            full((968, LANES)),
            full((968, LANES)),
        ],
        out_shape=[
            jax.ShapeDtypeStruct((5, NB, NZ, LANES), F32),
            jax.ShapeDtypeStruct((656, LANES), F32),
            jax.ShapeDtypeStruct((968, LANES), F32),
            jax.ShapeDtypeStruct((968, LANES), F32),
        ],
        cost_estimate=pl.CostEstimate(flops=10_000_000, bytes_accessed=12_000_000, transcendentals=0),
        name="pack",
    )(fields.reshape(5, NZ * NB, LANES), ocean, depth)


def adjoint_kernel(rows, c_ref, ocean_ref, depth_ref, fh_ref, fl_ref, *outs):
    src = outs[rows]
    r = lax.axis_index("rows")
    ids = level_ids()
    depth = depth_of(ocean_ref[...], depth_ref[...])
    for half in range(4):
        for yi in range(8):
            y = half * 8 + yi
            w = jnp.where(ids < depth[y : y + 1, :], c_ref[0, pl.ds(y, NZ, stride=NB), :], 0.0)
            src[:, yi * LANES : (yi + 1) * LANES] = TIME_STEP * dz(w, ids)
        hi, lo = split(src[...])
        res = dot3(fh_ref[r], fl_ref[r], hi, lo)
        size = NZ // rows
        for s in range(rows):
            for yi in range(8):
                outs[s][half * 8 + yi] = res[s * size : (s + 1) * size, yi * LANES : (yi + 1) * LANES]


def adjoint_source(cotangent, ocean, depth, fwd, rows):
    size = NZ // rows
    return pl.pallas_call(
        functools.partial(adjoint_kernel, rows),
        grid=(1,),
        in_specs=[
            pl.BlockSpec((1, NZ * NB, LANES), lambda i: (2, 0, 0)),
            pl.BlockSpec((NB, LANES), lambda i: (0, 0)),
            pl.BlockSpec((NB, LANES), lambda i: (0, 0)),
            pl.BlockSpec((rows, NZ, NZ), lambda i: (0, 0, 0)),
            pl.BlockSpec((rows, NZ, NZ), lambda i: (0, 0, 0)),
        ],
        out_specs=[pl.BlockSpec((NB, size, LANES), lambda i: (0, 0, 0))] * rows,
        out_shape=[jax.ShapeDtypeStruct((NB, size, LANES), F32)] * rows,
        scratch_shapes=[pltpu.VMEM((NZ, 8 * LANES), F32)],
        cost_estimate=pl.CostEstimate(flops=10_000_000, bytes_accessed=2_100_000, transcendentals=0),
        name="adjoint",
    )(cotangent.reshape(5, NZ * NB, LANES), ocean, depth, *fwd)


def corrected(pos, speed, mag, y1, y2, y3, y4, y5, qm, qp):
    x1 = jnp.where(pos, y1, y5)
    x2 = jnp.where(pos, y2, y4)
    x3 = y3
    x4 = jnp.where(pos, y4, y2)
    c = jnp.where(pos, qm, qp)
    d1 = x2 - x1
    d2 = x3 - x2
    d3 = x4 - x3
    x3d = x3 + x3
    t0 = d1 + (x2 + x2)
    t1 = x2 + x3
    t2 = d3 - x3d
    eps4 = 4.0 * WENO_EPS
    e0 = (eps4 + t0 * t0) + (13.0 / 3.0) * (d1 * d1)
    e1 = (eps4 + t1 * t1) + (13.0 / 3.0) * (d2 * d2)
    e2 = (eps4 + t2 * t2) + (13.0 / 3.0) * (d3 * d3)
    f0 = e1 * e2
    f1 = e0 * e2
    f2 = e0 * e1
    g0 = f0 * f0
    g1 = 6.0 * (f1 * f1)
    g2 = 3.0 * (f2 * f2)
    k0 = t0 + d1 + x2
    k1 = t1 + x3
    k2 = x3d - d3 + x3
    num = g0 * k0 + g1 * k1 + g2 * k2
    den = g0 + g1 + g2
    return speed * c + mag * (num / den)


def advect_kernel(ft_ref, own_ref, east_ref, west_ref, south_ref, north_ref, depth_ref, ocean_ref,
                  adv_ref, spread_ref, ext, dd, dfx, dfy, dfp, exy, fxe):
    zb = pl.program_id(0)
    z0 = pl.multiple_of(zb * 8, 8)
    zf = (lax.broadcasted_iota(jnp.int32, (8, LANES), 0) + z0).astype(F32)
    lane = lax.broadcasted_iota(jnp.int32, (8, LANES), 1)
    in_hi = lax.rem(lane, 8) < 4
    first, second = lane == 0, lane <= 1
    last, last2 = lane == LANES - 1, lane >= LANES - 2

    @pl.when(zb == 0)
    def _():
        depth = depth_of(ocean_ref[...], depth_ref[...]).astype(F32)
        before = south_ref[960:968]
        for y in range(NB):
            g, yi = y // 16, y % 16
            d8 = jnp.broadcast_to(depth[y : y + 1], (8, LANES))
            at_d = pl.ds(640 + g * 8, 8)
            ed = jnp.where(in_hi, east_ref[at_d], west_ref[at_d])
            ed = pltpu.roll(ed, LANES - 8 * yi, 1) if yi else ed
            dd[y] = d8
            dfy[y] = jnp.minimum(before, d8)
            dfx[y] = jnp.minimum(d8, pltpu.roll(jnp.where(last, ed, d8), 1, 1))
            before = d8
        dfy[NB] = jnp.minimum(before, north_ref[960:968])
        for g in range(2):
            at_d = pl.ds(640 + g * 8, 8)
            d_face = jnp.where(in_hi, east_ref[at_d], own_ref[at_d])
            dfp[g] = jnp.minimum(d_face, pltpu.roll(d_face, 1, 1))

    for f in range(5):
        for r in range(3):
            at = pl.ds(pl.multiple_of((f * 3 + r) * NZ + z0, 8), 8)
            ext[f, r] = south_ref[at]
            ext[f, 3 + NB + r] = north_ref[at]
        ext[f, 3 : 3 + NB] = ft_ref[f]

    for g in range(2):
        d_face = dfp[g]
        for f in range(5):
            at = pl.ds(pl.multiple_of((f * 2 + g) * NZ + z0, 8), 8)
            exy[f, g] = jnp.where(in_hi, east_ref[at], west_ref[at])
            q = jnp.where(in_hi, east_ref[at], own_ref[at])
            qm = pltpu.roll(q, 1, 1)
            if f == 0:
                speed = jnp.where(zf < d_face, 0.5 * (q + qm), 0.0)
                pos = speed > 0
                mag = jnp.abs(speed) * (1.0 / 6.0)
            d = q - qm
            fxe[f, g] = corrected(
                pos, speed, mag, pltpu.roll(d, 2, 1), pltpu.roll(d, 1, 1), d,
                pltpu.roll(d, LANES - 1, 1), pltpu.roll(d, LANES - 2, 1), qm, q,
            )

    def face_y(j):
        d_face = dfy[j]
        out = []
        v = [ext[1, j + 2], ext[1, j + 3]]
        speed = jnp.where(zf < d_face, 0.5 * (v[0] + v[1]), 0.0)
        pos = speed > 0
        mag = jnp.abs(speed) * (1.0 / 6.0)
        dv = None
        for f in range(5):
            q = [ext[f, j + o] for o in range(6)]
            d = [q[o + 1] - q[o] for o in range(5)]
            if f == 1:
                dv = d[2]
            out.append(corrected(pos, speed, mag, d[0], d[1], d[2], d[3], d[4], q[2], q[3]))
        return out, dv

    def step(j, carry):
        below_flux, below_dv = carry
        above_flux, above_dv = face_y(j + 1)
        g = j // 16
        yi = lax.rem(j, 16)
        back = lax.rem(LANES - 8 * yi, LANES)
        to_last = LANES - 1 - 8 * yi
        d_face = dfx[j]
        wet = zf < dd[j]
        du = None
        for f in range(5):
            q = ext[f, j + 3]
            e = pltpu.roll(exy[f, g], back, 1)
            qm = pltpu.roll(jnp.where(last, e, q), 1, 1)
            em = pltpu.roll(jnp.where(last, q, e), 1, 1)
            d = q - qm
            de = e - em
            if f == 0:
                speed = jnp.where(zf < d_face, 0.5 * (q + qm), 0.0)
                pos = speed > 0
                mag = jnp.abs(speed) * (1.0 / 6.0)
            y1 = pltpu.roll(jnp.where(last2, de, d), 2, 1)
            y2 = pltpu.roll(jnp.where(last, de, d), 1, 1)
            y4 = pltpu.roll(jnp.where(first, de, d), LANES - 1, 1)
            y5 = pltpu.roll(jnp.where(second, de, d), LANES - 2, 1)
            if f == 0:
                du = d + y4
            flux = corrected(pos, speed, mag, y1, y2, d, y4, y5, qm, q)
            east = jnp.where(last, pltpu.roll(fxe[f, g], to_last, 1), pltpu.roll(flux, LANES - 1, 1))
            total = (flux - east) + (below_flux[f] - above_flux[f])
            adv_ref[f, j] = jnp.where(wet, q + TIME_STEP * total, 0.0)
        spread_ref[j] = 0.5 * du + 0.5 * (below_dv + above_dv)
        return above_flux, above_dv

    lax.fori_loop(0, NB, step, face_y(0), unroll=4)


def advect(ft, own, east, west, south, north, depth, ocean):
    full = lambda shape: pl.BlockSpec(shape, lambda i: (0,) * len(shape))
    return pl.pallas_call(
        advect_kernel,
        grid=(NZ // 8,),
        in_specs=[
            pl.BlockSpec((5, NB, 8, LANES), lambda i: (0, 0, i, 0)),
            full((656, LANES)), full((656, LANES)), full((656, LANES)),
            full((968, LANES)), full((968, LANES)),
            full((NB, LANES)), full((NB, LANES)),
        ],
        out_specs=[
            pl.BlockSpec((5, NB, 8, LANES), lambda i: (0, 0, i, 0)),
            pl.BlockSpec((NB, 8, LANES), lambda i: (0, i, 0)),
        ],
        out_shape=[
            jax.ShapeDtypeStruct((5, NB, NZ, LANES), F32),
            jax.ShapeDtypeStruct((NB, NZ, LANES), F32),
        ],
        scratch_shapes=[
            pltpu.VMEM((5, NB + 6, 8, LANES), F32),
            pltpu.VMEM((NB, 8, LANES), F32),
            pltpu.VMEM((NB, 8, LANES), F32),
            pltpu.VMEM((NB + 1, 8, LANES), F32),
            pltpu.VMEM((2, 8, LANES), F32),
            pltpu.VMEM((5, 2, 8, LANES), F32),
            pltpu.VMEM((5, 2, 8, LANES), F32),
        ],
        cost_estimate=pl.CostEstimate(flops=200_000_000, bytes_accessed=130_000_000, transcendentals=0),
        name="advect",
    )(ft, own, east, west, south, north, depth, ocean)


def forward_kernel(rows, adv_ref, w_ref, spread_ref, depth_ref, ocean_ref, win_ref, bin_ref, wout_ref,
                   fh_ref, fl_ref, *refs):
    pieces = refs[:rows]
    rates_ref, act_ref, hs_ref, feats, rate_s, src = refs[rows:]
    r = lax.axis_index("rows")
    ids = level_ids()
    depth = depth_of(ocean_ref[...], depth_ref[...])
    for n, f in enumerate((0, 1, 3, 4)):
        for yi in range(8):
            feats[n * NZ : (n + 1) * NZ, yi * LANES : (yi + 1) * LANES] = adv_ref[f, yi].astype(BF16)
    pre = lax.dot_general(win_ref[...], feats[...], (((0,), (0,)), ((), ())), preferred_element_type=F32)
    act = jnp.tanh(pre + bin_ref[...])
    act_ref[0] = act
    out = lax.dot_general(wout_ref[...], act.astype(BF16), (((0,), (0,)), ((), ())), preferred_element_type=F32)
    rate_s[...] = 2.0 * jax.nn.sigmoid(out)
    for yi in range(8):
        cols = slice(yi * LANES, (yi + 1) * LANES)
        row = depth[yi : yi + 1, :]
        wet = ids < row
        rates = rate_s[:, cols]
        rates_ref[yi] = rates
        mixed = []
        for n, f in enumerate((3, 4)):
            t = adv_ref[f, yi]
            flux = jnp.where(ids + 1 < row, rates * (above(t) - t), 0.0)
            m = jnp.where(wet, t + TIME_STEP * (flux - below(flux)), 0.0)
            hs_ref[n, yi] = m
            mixed.append(m)
        density = 0.5 * mixed[0] - 0.5 * mixed[1]
        rhs = dz(density, ids) - (spread_ref[yi] + dz(w_ref[0, yi], ids)) / TIME_STEP
        src[:, cols] = jnp.where(wet, rhs, 0.0)
    hi, lo = split(src[...])
    res = dot3(fh_ref[r], fl_ref[r], hi, lo)
    size = NZ // rows
    for s in range(rows):
        for yi in range(8):
            pieces[s][yi] = res[s * size : (s + 1) * size, yi * LANES : (yi + 1) * LANES]


def closure_forward(adv, ft, spread, depth, ocean, win, b_in, wout, fwd, rows):
    size = NZ // rows
    full = lambda shape: pl.BlockSpec(shape, lambda i: (0,) * len(shape))
    plane = pl.BlockSpec((8, LANES), lambda i: (i, 0))
    ycol = pl.BlockSpec((8, NZ, LANES), lambda i: (i, 0, 0))
    return pl.pallas_call(
        functools.partial(forward_kernel, rows),
        grid=(NB // 8,),
        in_specs=[
            pl.BlockSpec((5, 8, NZ, LANES), lambda i: (0, i, 0, 0)),
            pl.BlockSpec((1, 8, NZ, LANES), lambda i: (2, i, 0, 0)),
            ycol, plane, plane,
            full((256, 256)), full((256, 1)), full((256, NZ)),
            full((rows, NZ, NZ)), full((rows, NZ, NZ)),
        ],
        out_specs=[pl.BlockSpec((8, size, LANES), lambda i: (i, 0, 0))] * rows
        + [ycol, pl.BlockSpec((1, 256, 1024), lambda i: (i, 0, 0)),
           pl.BlockSpec((2, 8, NZ, LANES), lambda i: (0, i, 0, 0))],
        out_shape=[jax.ShapeDtypeStruct((NB, size, LANES), F32)] * rows
        + [
            jax.ShapeDtypeStruct((NB, NZ, LANES), F32),
            jax.ShapeDtypeStruct((NB // 8, 256, 1024), F32),
            jax.ShapeDtypeStruct((2, NB, NZ, LANES), F32),
        ],
        scratch_shapes=[
            pltpu.VMEM((256, 1024), BF16),
            pltpu.VMEM((NZ, 1024), F32),
            pltpu.VMEM((NZ, 1024), F32),
        ],
        cost_estimate=pl.CostEstimate(flops=900_000_000, bytes_accessed=18_000_000, transcendentals=1_500_000),
        name="closure_forward",
    )(adv, ft, spread, depth, ocean, win, b_in, wout, *fwd)


def root_of(d):
    q = jnp.sqrt(d + 0.25 * d * d)
    return 1.0 / (1.0 + 0.5 * d + q), 0.5 / q


def exchange_rows(rows, cols, chunk):
    n = NZ // cols
    tile = max(8, 2 * n)
    start = (chunk // n) * tile + chunk % n
    return start, (rows // n) * tile, n, tile


def line_kernel(rows, cols, *refs):
    pieces = refs[:rows]
    ch_ref, cl_ref, lv_ref, ex_ref, v_ref, s_ref, work = refs[rows:]
    r = lax.axis_index("rows")
    size = NZ // rows
    wide = rows * LANES
    total = None
    for s in range(rows):
        src = lax.rem(r - s + rows, rows)
        at = pl.ds(pl.multiple_of(src * LANES, LANES), LANES)
        hi, lo = split(pieces[s][...])
        part = dot3(hi, lo, ch_ref[at, :], cl_ref[at, :])
        total = part if total is None else total + part
    work[...] = total
    d = lv_ref[pl.ds(pl.multiple_of(r * size, size), size), :] + ex_ref[...]
    lam, _ = root_of(d)

    def causal(y, c):
        at = pl.ds(pl.multiple_of(y * size, size), size)
        c = work[at] + lam * c
        v_ref[at] = c
        return c

    end = lax.fori_loop(0, NB, causal, jnp.zeros((size, wide), F32))

    def anticausal(i, a):
        at = pl.ds(pl.multiple_of((NB - 1 - i) * size, size), size)
        x = work[at]
        v_ref[at] = v_ref[at] + lam * a
        return x + lam * a

    start = lax.fori_loop(0, NB, anticausal, jnp.zeros((size, wide), F32))
    s_ref[...] = jnp.zeros_like(s_ref)
    for ch in range(rows):
        row, stride, n, _ = exchange_rows(rows, cols, ch)
        lanes = slice(ch * LANES, (ch + 1) * LANES)
        s_ref[pl.ds(row, size, stride=stride), :] = start[:, lanes]
        s_ref[pl.ds(row + n, size, stride=stride), :] = end[:, lanes]


def line_solve(pieces, tables, rows, cols):
    size = NZ // rows
    wide = rows * LANES
    tile = exchange_rows(rows, cols, 0)[3]
    return pl.pallas_call(
        functools.partial(line_kernel, rows, cols),
        in_specs=[VM] * (rows + 4),
        out_specs=[VM, VM],
        out_shape=[
            jax.ShapeDtypeStruct((NB * size, wide), F32),
            jax.ShapeDtypeStruct((cols * tile, LANES), F32),
        ],
        scratch_shapes=[pltpu.VMEM((NB * size, wide), F32)],
        cost_estimate=pl.CostEstimate(flops=800_000_000, bytes_accessed=4_500_000, transcendentals=0),
        name="line_solve",
    )(*[p.reshape(NB * size, LANES) for p in pieces], *tables)


def carry_kernel(rows, cols, s_ref, lv_ref, ex_ref, c_ref, got, send, up, down, dsem, send_sem, recv_sem):
    n = NZ // cols
    tile = max(8, 2 * n)
    me = lax.axis_index("cols")
    r = lax.axis_index("rows")
    barrier = pltpu.get_barrier_semaphore()

    def greet(t, carry):
        pl.semaphore_signal(barrier, inc=1, device_id={"cols": lax.rem(me + t, cols)}, device_id_type=MESH)
        return carry

    lax.fori_loop(1, cols, greet, 0)
    pl.semaphore_wait(barrier, cols - 1)

    def out_copy(t):
        peer = lax.rem(me + t, cols)
        return pltpu.make_async_remote_copy(
            src_ref=s_ref.at[peer], dst_ref=got.at[me], send_sem=send_sem.at[0], recv_sem=recv_sem.at[0],
            device_id={"cols": peer}, device_id_type=MESH,
        )

    def back_copy(t):
        peer = lax.rem(me + t, cols)
        return pltpu.make_async_remote_copy(
            src_ref=send.at[peer], dst_ref=c_ref.at[me], send_sem=send_sem.at[1], recv_sem=recv_sem.at[1],
            device_id={"cols": peer}, device_id_type=MESH,
        )

    def run(make):
        lax.fori_loop(1, cols, lambda t, c: (make(t).start(), c)[1], 0)

    def finish(i):
        others = got.at[pl.ds(0, cols - 1)]
        pltpu.make_async_copy(others, others, recv_sem.at[i]).wait()
        pltpu.make_async_copy(others, others, send_sem.at[i]).wait()

    run(out_copy)
    mine = pltpu.make_async_copy(s_ref.at[me], got.at[me], dsem.at[0])
    mine.start()
    size = NZ // rows
    level = r * size + (me * n) // rows
    chunk = lax.rem(me, rows // n)
    lam, _ = root_of(lv_ref[level] + ex_ref[chunk])
    mu = lam
    for _ in range(NB.bit_length() - 1):
        mu = mu * mu
    whole = mu
    for _ in range(cols.bit_length() - 1):
        whole = whole * whole
    scale = 1.0 / (1.0 - whole * whole)
    is_start = lax.broadcasted_iota(jnp.int32, (tile, LANES), 0) < n
    mine.wait()
    finish(0)

    zero = jnp.zeros((tile, LANES), F32)
    sa, sb = lax.fori_loop(
        0, cols, lambda k, c: (got[cols - 1 - k] + mu * c[0], got[k] + mu * c[1]), (zero, zero), unroll=8
    )
    left = (pltpu.roll(sa, n, 0) + whole * sb) * scale
    right = (pltpu.roll(sb, tile - n, 0) + whole * sa) * scale

    def both(k, c):
        m = cols - 1 - k
        up[k] = c[0]
        down[m] = c[1]
        return got[k] + mu * c[0], got[m] + mu * c[1]

    lax.fori_loop(0, cols, both, (left, right), unroll=8)
    send[...] = jnp.where(is_start, down[...], up[...])
    run(back_copy)
    mine2 = pltpu.make_async_copy(send.at[me], c_ref.at[me], dsem.at[1])
    mine2.start()
    mine2.wait()
    finish(1)


def carries(moments, rows, cols, cid):
    _, _, n, tile = exchange_rows(rows, cols, 0)
    level_list = jnp.asarray(SPECTRAL_SHIFT + eigen_np(NZ), F32)
    east = eigen_np(rows * LANES).reshape(rows // n, n, LANES)
    east_tiles = jnp.asarray(east[:, np.arange(tile) % n], F32)
    return pl.pallas_call(
        functools.partial(carry_kernel, rows, cols),
        in_specs=[VM, pl.BlockSpec(memory_space=pltpu.SMEM), VM],
        out_specs=VM,
        out_shape=jax.ShapeDtypeStruct((cols, tile, LANES), F32),
        scratch_shapes=[
            pltpu.VMEM((cols, tile, LANES), F32),
            pltpu.VMEM((cols, tile, LANES), F32),
            pltpu.VMEM((cols, tile, LANES), F32),
            pltpu.VMEM((cols, tile, LANES), F32),
            pltpu.SemaphoreType.DMA((2,)),
            pltpu.SemaphoreType.DMA((2,)),
            pltpu.SemaphoreType.DMA((2,)),
        ],
        compiler_params=pltpu.CompilerParams(collective_id=cid, has_side_effects=True),
        name="carries",
    )(moments.reshape(cols, tile, LANES), level_list, east_tiles)


def back_kernel(rows, cols, v_ref, c_ref, ch_ref, cl_ref, lv_ref, ex_ref, *refs):
    outs = refs[:rows]
    work = refs[rows]
    r = lax.axis_index("rows")
    size = NZ // rows
    d = lv_ref[pl.ds(pl.multiple_of(r * size, size), size), :] + ex_ref[...]
    lam, kappa = root_of(d)
    left, right = [], []
    for ch in range(rows):
        row, stride, n, _ = exchange_rows(rows, cols, ch)
        right.append(c_ref[pl.ds(row, size, stride=stride), :])
        left.append(c_ref[pl.ds(row + n, size, stride=stride), :])
    left = jnp.concatenate(left, 1) * (lam * kappa)
    right = jnp.concatenate(right, 1) * (lam * kappa)

    def fwd(y, h):
        at = pl.ds(pl.multiple_of(y * size, size), size)
        work[at] = kappa * v_ref[at] + h
        return lam * h

    lax.fori_loop(0, NB, fwd, left)

    def bwd(i, h):
        at = pl.ds(pl.multiple_of((NB - 1 - i) * size, size), size)
        work[at] = work[at] + h
        return lam * h

    lax.fori_loop(0, NB, bwd, right)
    hi, lo = split(work[...])
    for s in range(rows):
        dst = lax.rem(r + s, rows)
        outs[s][...] = dot3(hi, lo, ch_ref[dst], cl_ref[dst])


def line_back(v, c, tables, rows, cols):
    size = NZ // rows
    outs = pl.pallas_call(
        functools.partial(back_kernel, rows, cols),
        in_specs=[VM] * 6,
        out_specs=[VM] * rows,
        out_shape=[jax.ShapeDtypeStruct((NB * size, LANES), F32)] * rows,
        scratch_shapes=[pltpu.VMEM((NB * size, rows * LANES), F32)],
        cost_estimate=pl.CostEstimate(flops=800_000_000, bytes_accessed=4_500_000, transcendentals=0),
        name="line_back",
    )(v, c.reshape(-1, LANES), *tables)
    return [o.reshape(NB, size, LANES) for o in outs]


def gather_levels(pieces, rows, buf, base=0):
    size = NZ // rows
    for s in range(rows):
        for yi in range(8):
            buf[s * size : (s + 1) * size, yi * LANES : (yi + 1) * LANES] = pieces[s][base + yi]


def backward_kernel(rows, *refs):
    pieces = refs[:rows]
    (adv_ref, ct_ref, cs_ref, rates_ref, act_ref, depth_ref, ocean_ref, wout_ref, ih_ref, il_ref,
     g_ref, buf, feats, gos, gw, gwo, gb) = refs[rows:]
    i = pl.program_id(0)
    r = lax.axis_index("rows")
    ids = level_ids()
    depth = depth_of(ocean_ref[...], depth_ref[...])
    gather_levels(pieces, rows, buf)
    hi, lo = split(buf[...])
    buf[...] = dot3(ih_ref[r], il_ref[r], hi, lo)
    for n, f in enumerate((0, 1, 3, 4)):
        for yi in range(8):
            feats[n * NZ : (n + 1) * NZ, yi * LANES : (yi + 1) * LANES] = adv_ref[f, yi].astype(BF16)
    for yi in range(8):
        cols = slice(yi * LANES, (yi + 1) * LANES)
        row = depth[yi : yi + 1, :]
        wet = ids < row
        grad_density = -dz(jnp.where(wet, buf[:, cols], 0.0), ids)
        rates = rates_ref[yi]
        total = None
        for f, c_ref, sign in ((3, ct_ref, 0.5), (4, cs_ref, -0.5)):
            grad = c_ref[0, pl.ds(yi, NZ, stride=8), :] + sign * grad_density
            grad = jnp.where(wet, grad, 0.0)
            t = adv_ref[f, yi]
            term = (grad - above(grad)) * (above(t) - t)
            total = term if total is None else total + term
        grad_rates = jnp.where(ids + 1 < row, TIME_STEP * total, 0.0)
        gos[:, cols] = (grad_rates * rates * (1.0 - 0.5 * rates)).astype(BF16)
    act = act_ref[0]
    go = gos[...]
    gpre = jnp.dot(wout_ref[...], go, preferred_element_type=F32) * (1.0 - act * act)
    p_hi, p_lo = split(gpre)
    ones = jnp.ones((8, 1024), BF16)

    @pl.when(i == 0)
    def _():
        gw[...] = jnp.zeros_like(gw)
        gwo[...] = jnp.zeros_like(gwo)
        gb[...] = jnp.zeros_like(gb)

    gw[...] += dot_nt(feats[...], p_hi)
    gwo[...] += dot_nt(go, act.astype(BF16))
    gb[...] += dot_nt(ones, p_hi) + dot_nt(ones, p_lo)

    @pl.when(i == NB // 8 - 1)
    def _():
        for h in range(2):
            lanes = slice(h * LANES, (h + 1) * LANES)
            g_ref[h * 256 : (h + 1) * 256] = gw[:, lanes]
            g_ref[512 + h * NZ : 512 + (h + 1) * NZ] = gwo[:, lanes]
            g_ref[575 + h * NZ : 576 + h * NZ] = gb[0:1, lanes]
        g_ref[640:1024] = jnp.zeros((384, LANES), F32)


def closure_backward(pieces, adv, cotangent, rates, act, depth, ocean, wout, inv, rows):
    size = NZ // rows
    full = lambda shape: pl.BlockSpec(shape, lambda i: (0,) * len(shape))
    plane = pl.BlockSpec((8, LANES), lambda i: (i, 0))
    ycol = pl.BlockSpec((8, NZ, LANES), lambda i: (i, 0, 0))
    cot = cotangent.reshape(5, NZ, NB // 8, 8, LANES)

    def kernel(*refs):
        refs = list(refs)
        for at in (rows + 1, rows + 2):
            refs[at] = refs[at].reshape(1, NZ * 8, LANES)
        backward_kernel(rows, *refs)

    cot_spec = lambda f: pl.BlockSpec((1, NZ, 1, 8, LANES), lambda i: (f, 0, i, 0, 0))
    return pl.pallas_call(
        kernel,
        grid=(NB // 8,),
        in_specs=[pl.BlockSpec((8, size, LANES), lambda i: (i, 0, 0))] * rows
        + [
            pl.BlockSpec((5, 8, NZ, LANES), lambda i: (0, i, 0, 0)),
            cot_spec(3), cot_spec(4), ycol,
            pl.BlockSpec((1, 256, 1024), lambda i: (i, 0, 0)),
            plane, plane, full((256, NZ)), full((rows, NZ, NZ)), full((rows, NZ, NZ)),
        ],
        out_specs=full((1024, LANES)),
        out_shape=jax.ShapeDtypeStruct((1024, LANES), F32),
        scratch_shapes=[
            pltpu.VMEM((NZ, 1024), F32),
            pltpu.VMEM((256, 1024), BF16),
            pltpu.VMEM((NZ, 1024), BF16),
            pltpu.VMEM((256, 256), F32),
            pltpu.VMEM((NZ, 256), F32),
            pltpu.VMEM((8, 256), F32),
        ],
        cost_estimate=pl.CostEstimate(flops=1_200_000_000, bytes_accessed=16_000_000, transcendentals=0),
        name="closure_backward",
    )(*pieces, adv, cot, cot, rates, act, depth, ocean, wout, *inv)


def sum_kernel(rows, cols, g_ref, o_ref, land, acc, land2, total, tile_ref, dsem, send_sem, recv_sem):
    me = lax.axis_index("cols")
    r = lax.axis_index("rows")
    barrier = pltpu.get_barrier_semaphore()

    def greet(t, carry):
        pl.semaphore_signal(barrier, inc=1, device_id={"cols": lax.rem(me + t, cols)}, device_id_type=MESH)
        return carry

    lax.fori_loop(1, cols, greet, 0)
    for t in range(1, rows):
        pl.semaphore_signal(barrier, inc=1, device_id={"rows": lax.rem(r + t, rows)}, device_id_type=MESH)
    pl.semaphore_wait(barrier, cols - 1 + rows - 1)

    def copy(axis, count, at, t, src, dst, i):
        return pltpu.make_async_remote_copy(
            src_ref=src, dst_ref=dst, send_sem=send_sem.at[i], recv_sem=recv_sem.at[i],
            device_id={axis: lax.rem(at + t, count)}, device_id_type=MESH,
        )

    def rows_out(t):
        return copy("rows", rows, r, t, g_ref.at[lax.rem(r + t, rows)], land.at[t], 0)

    def cols_out(t):
        return copy("cols", cols, me, t, acc.at[lax.rem(me + t, cols)], land2.at[t], 1)

    def cols_back(t):
        return copy("cols", cols, me, t, tile_ref, total.at[me], 2)

    def rows_back(t):
        return copy("rows", rows, r, t, total, o_ref.at[r], 3)

    def all_of(make, count, ref, i):
        lax.fori_loop(1, count, lambda t, c: (make(t).start(), c)[1], 0)
        others = ref.at[pl.ds(0, count - 1)]
        pltpu.make_async_copy(others, others, recv_sem.at[i]).wait()
        pltpu.make_async_copy(others, others, send_sem.at[i]).wait()

    all_of(rows_out, rows, land, 0)
    value = g_ref[r]
    for t in range(1, rows):
        value = value + land[t]
    acc[...] = value
    all_of(cols_out, cols, land2, 1)
    value = lax.fori_loop(1, cols, lambda t, v: v + land2[t], acc[me])
    tile_ref[...] = value
    total[me] = value
    all_of(cols_back, cols, land2, 2)
    own = pltpu.make_async_copy(total, o_ref.at[r], dsem.at[0])
    own.start()
    all_of(rows_back, rows, land, 3)
    own.wait()


def sum_gradients(g, rows, cols, cid):
    tile = 1024 // (rows * cols)
    return pl.pallas_call(
        functools.partial(sum_kernel, rows, cols),
        in_specs=[VM],
        out_specs=VM,
        out_shape=jax.ShapeDtypeStruct((rows, cols, tile, LANES), F32),
        scratch_shapes=[
            pltpu.VMEM((rows, cols, tile, LANES), F32),
            pltpu.VMEM((cols, tile, LANES), F32),
            pltpu.VMEM((cols, tile, LANES), F32),
            pltpu.VMEM((cols, tile, LANES), F32),
            pltpu.VMEM((tile, LANES), F32),
            pltpu.SemaphoreType.DMA((1,)),
            pltpu.SemaphoreType.DMA((4,)),
            pltpu.SemaphoreType.DMA((4,)),
        ],
        compiler_params=pltpu.CompilerParams(collective_id=cid, has_side_effects=True),
        name="sum_gradients",
    )(g.reshape(rows, cols, tile, LANES)).reshape(1024, LANES)


def place_kernel(adv_ref, hs_ref, o_ref):
    i = pl.program_id(0)

    @pl.when(i < 2)
    def _():
        for y in range(NB):
            o_ref[0, pl.ds(y, NZ, stride=NB), :] = adv_ref[0, y]

    @pl.when(i >= 2)
    def _():
        for y in range(NB):
            o_ref[0, pl.ds(y, NZ, stride=NB), :] = hs_ref[0, y]


def place(adv, hs):
    block = lambda index: pl.BlockSpec((1, NB, NZ, LANES), index)
    return pl.pallas_call(
        place_kernel,
        grid=(4,),
        in_specs=[
            block(lambda i: (jnp.minimum(i, 1), 0, 0, 0)),
            block(lambda i: (jnp.maximum(i - 2, 0), 0, 0, 0)),
        ],
        out_specs=pl.BlockSpec((1, NZ * NB, LANES), lambda i: (i + (i >= 2), 0, 0)),
        out_shape=jax.ShapeDtypeStruct((5, NZ * NB, LANES), F32),
        cost_estimate=pl.CostEstimate(flops=1_000_000, bytes_accessed=8_400_000, transcendentals=0),
        name="place",
    )(adv, hs)


def finish_kernel(rows, *refs):
    pieces = refs[:rows]
    adv_ref, depth_ref, ocean_ref, ih_ref, il_ref, _, o_ref, p_ref, buf = refs[rows:]
    r = lax.axis_index("rows")
    ids = level_ids()
    depth = depth_of(ocean_ref[...], depth_ref[...])
    for part in range(NB // 8):
        gather_levels(pieces, rows, buf, part * 8)
        hi, lo = split(buf[...])
        pressure = dot3(ih_ref[r], il_ref[r], hi, lo)
        for yi in range(8):
            y = part * 8 + yi
            p = pressure[:, yi * LANES : (yi + 1) * LANES]
            p_ref[pl.ds(y, NZ, stride=NB), :] = p
            new_w = jnp.where(ids < depth[y : y + 1, :], adv_ref[0, y] - TIME_STEP * dz(p, ids), 0.0)
            o_ref[0, pl.ds(y, NZ, stride=NB), :] = new_w


def finish(pieces, adv, depth, ocean, inv, placed, rows):
    size = NZ // rows
    full = lambda shape: pl.BlockSpec(shape, lambda i: (0,) * len(shape))
    return pl.pallas_call(
        functools.partial(finish_kernel, rows),
        grid=(1,),
        in_specs=[full((NB, size, LANES))] * rows
        + [
            pl.BlockSpec((1, NB, NZ, LANES), lambda i: (2, 0, 0, 0)),
            full((NB, LANES)), full((NB, LANES)), full((rows, NZ, NZ)), full((rows, NZ, NZ)), ANY,
        ],
        out_specs=[pl.BlockSpec((1, NZ * NB, LANES), lambda i: (2, 0, 0)), full((NZ * NB, LANES))],
        out_shape=[
            jax.ShapeDtypeStruct((5, NZ * NB, LANES), F32),
            jax.ShapeDtypeStruct((NZ * NB, LANES), F32),
        ],
        scratch_shapes=[pltpu.VMEM((NZ, 1024), F32)],
        input_output_aliases={rows + 5: 0},
        cost_estimate=pl.CostEstimate(flops=50_000_000, bytes_accessed=4_200_000, transcendentals=0),
        name="finish",
    )(*pieces, adv, depth, ocean, *inv, placed)


def shift_pieces(pieces, rows):
    got = [pieces[0]]
    for s in range(1, rows):
        got.append(lax.ppermute(pieces[s], "rows", [(i, (i + s) % rows) for i in range(rows)]))
    return got


def per_device(rows, cols, fields, cotangent, ocean, depth, in_weight, in_bias, out_weight):
    fwd, inv = level_tables(rows)
    east_np = dct_np(rows * LANES)
    east_fwd = hi_lo_np(east_np.T)
    east_inv = hi_lo_np(np.stack(np.split(east_np, rows, axis=1)))
    levels = jnp.asarray(np.repeat((SPECTRAL_SHIFT + eigen_np(NZ))[:, None], rows * LANES, 1), F32)
    easts = jnp.asarray(eigen_np(rows * LANES)[None, :], F32)
    b_in = in_bias[:, None]
    wout = jnp.pad(out_weight, ((0, 0), (0, 1)))

    ft, own, lo, hi = pack(fields, ocean, depth)
    up_r = [(i, i + 1) for i in range(rows - 1)]
    up_c = [(i, i + 1) for i in range(cols - 1)]
    down_r = [(b, a) for a, b in up_r]
    down_c = [(b, a) for a, b in up_c]
    south = lax.ppermute(hi, "cols", up_c)
    north = lax.ppermute(lo, "cols", down_c)
    west = lax.ppermute(own, "rows", up_r)
    east = lax.ppermute(own, "rows", down_r)

    adj = shift_pieces(adjoint_source(cotangent, ocean, depth, fwd, rows), rows)
    adv, spread = advect(ft, own, east, west, south, north, depth, ocean)

    v, moments = line_solve(adj, (*east_fwd, levels, easts), rows, cols)
    c = carries(moments, rows, cols, 1)
    adj = shift_pieces(line_back(v, c, (*east_inv, levels, easts), rows, cols), rows)

    *pieces, rates, act, hs = closure_forward(adv, ft, spread, depth, ocean, in_weight, b_in, wout, fwd, rows)
    pieces = shift_pieces(pieces, rows)
    grads = closure_backward(adj, adv, cotangent, rates, act, depth, ocean, wout, inv, rows)
    placed = place(adv, hs)

    v, moments = line_solve(pieces, (*east_fwd, levels, easts), rows, cols)
    c = carries(moments, rows, cols, 1)
    pieces = line_back(v, c, (*east_inv, levels, easts), rows, cols)
    grads, pieces[0] = lax.optimization_barrier((grads, pieces[0]))
    pieces = shift_pieces(pieces, rows)
    grads = sum_gradients(grads, rows, cols, 2)
    new_fields, pressure = finish(pieces, adv, depth, ocean, inv, placed, rows)

    g_in = jnp.concatenate([grads[0:256], grads[256:512]], 1)
    g_out = jnp.concatenate([grads[512:576], grads[576:640]], 1)
    return (
        new_fields.reshape(5, NZ, NB, LANES),
        pressure.reshape(NZ, NB, LANES),
        g_in,
        g_out[NZ - 1],
        g_out[: NZ - 1].T,
    )


def solution(mesh):
    rows, cols = mesh.shape["rows"], mesh.shape["cols"]
    in_specs = (
        P(None, None, "cols", "rows"),
        P(None, None, "cols", "rows"),
        P("cols", "rows"),
        P("cols", "rows"),
        P(),
        P(),
        P(),
    )
    out_specs = (P(None, None, "cols", "rows"), P(None, "cols", "rows"), P(), P(), P())
    return jax.shard_map(
        functools.partial(per_device, rows, cols),
        mesh=mesh, in_specs=in_specs, out_specs=out_specs, check_vma=False,
    )
```
